512 devices in a mesh: gen: 64 (over z_hi, y, core), tp: 8 (over x, z_lo).
Axes of the slice: x: 4, y: 8, z: 8 (z_hi: 4, z_lo: 2; z = z_hi * 2 + z_lo), core: 2. Of those that a mesh axis runs over, the one named last changes fastest.
Arguments:
- tokens_in: bfloat16 [8192, 5120], P('gen', 'tp'), may hold values from -6 to 6
- w_kv: bfloat16 [5120, 2048], P('tp'), may hold values from -0.078125 to 0.078125
- queries: bfloat16 [4096, 2, 40, 128], P('gen', None, 'tp'), may hold values from -8 to 8
- k_cache: bfloat16 [3584, 8, 64, 128], P('gen', 'tp'), may hold values from -8 to 8
- v_cache: bfloat16 [3584, 8, 64, 128], P('gen', 'tp'), may hold values from -5 to 5
- page_table: int32 [4096, 32], P('gen'), may hold values from 0 to 55, as said below
- lengths: int32 [4096], P('gen'), may hold values from 1 to 2048, as said below
- move_dest: int32 [4096, 1], replicated, may hold values from 0 to 63; in each aligned block of 64 rows (0 to 63, 64 to 127, ...) at most 2 rows name the same one
- move_page: int32 [4096], replicated, may hold values from 0 to 55
- move_seq: int32 [4096], replicated, may hold values from 0 to 63
Outputs:
- attended: bfloat16 [4096, 2, 40, 128], P('gen', None, 'tp')
- new_kv: bfloat16 [8192, 2048], P('gen', 'tp')
The draws below stay inside these ranges and needn't reach their ends.
Inputs may be any that keep to these rules, and one draw needn't show every extreme that they name: `page_table`: each row names 32 different pages. `lengths`: some sequence has exactly 2048 positions in every draw. `move_dest`: rows r * 64 to (r + 1) * 64 - 1 are the moves of source device r; among one source's rows no destination appears more than 2 times, a bound that some block reaches.
All inputs are finite; a program needn't handle non-finite values.
Results may differ from the reference program's by a relative error of at most 0.0043.
Values may be sent and summed in bfloat16 or wider, within the bound.
A program may use at most 128 MiB of HBM per device.

```python
import math
import jax
import jax.numpy as jnp
import numpy as np
from jax import lax

D = 5120
HEADS = 40
KV_HEADS = 8
HD = 128
GROUP = 5
SEQ_DEV = 64
STEPS = 2
PAGE = 64
MAXP = 32
POOL = 56
CAP = 2
SEQS = 4096
TOKENS = 8192
POOL_ALL = 3584
MOVES_DEV = 64
MOVES = 4096
N_GEN = 64


def draw_k_cache(key, part):
    full_shape = (POOL_ALL, KV_HEADS, PAGE, HD)
    values_drawn = jnp.clip(jax.random.normal(jax.random.fold_in(key, 1), full_shape, jnp.float32), -5.0, 5.0)
    return values_drawn.astype(jnp.bfloat16)


def draw_queries(key, part):
    full_shape = (SEQS, STEPS, HEADS, HD)
    values_drawn = jnp.clip(jax.random.normal(jax.random.fold_in(key, 2), full_shape, jnp.float32), -5.0, 5.0)
    return values_drawn.astype(jnp.bfloat16)


def draw_page_table(key, part):
    row_keys = jax.random.split(jax.random.fold_in(key, 11), SEQS)
    chosen = jax.vmap(lambda row_key: jax.random.permutation(row_key, POOL)[:MAXP])(row_keys)
    return chosen.astype(jnp.int32)


def draw_lengths(key, part):
    longest = MAXP * PAGE
    factor = jax.random.randint(jax.random.fold_in(key, 13), (SEQS // SEQ_DEV,), 1, 5)
    upper_limit = jnp.repeat(longest * factor // 4, SEQ_DEV, total_repeat_length=SEQS)
    drawn_lengths = jax.random.randint(jax.random.fold_in(key, 17), (SEQS,), 1, upper_limit + 1)
    full_index = jax.random.randint(jax.random.fold_in(key, 19), (), 0, SEQS)
    drawn_lengths = jnp.where(jnp.arange(SEQS) == full_index, longest, drawn_lengths)
    return drawn_lengths.astype(jnp.int32)


def with_ends(values, own_key, low, largest):
    longest = values.shape.index(max(values.shape))
    spots = []
    for shift in (0, 1):
        where = [jax.random.randint(jax.random.fold_in(own_key, axis), (), 0, length) for axis, length in enumerate(values.shape)]
        where[longest] = (where[longest] + shift) % values.shape[longest]
        spots.append(tuple(where))
    return values.at[spots[0]].set(low).at[spots[1]].set(largest)


def block_scale(rng, dims, cuts, low, top_value):
    def one(dim, parts):
        draws = jax.random.uniform(jax.random.fold_in(jax.random.fold_in(rng, 6), dim), (parts,), jnp.float32, low / len(cuts), top_value / len(cuts))
        return jnp.repeat(jnp.exp(draws), dims[dim] // parts).reshape((-1,) + (1,) * (len(dims) - dim - 1))

    level = one(*cuts[0])
    for cut in cuts[1:]:
        level = level * one(*cut)
    return level


def assign_block(own_key, own, number, rows, number_of, top, limit, lean):
    order = jax.random.permutation(own_key, number_of)
    crowded, usual = load_shares(number_of, rows * top, limit, lean, True), load_shares(number_of, rows * top, limit, lean, False)
    places = jnp.arange(number_of)

    def named(tallies, offset_by):
        used = int((tallies > 0).sum())
        fixed = max(1, used // 4)
        moved = fixed + (places - fixed + offset_by * (used - fixed)) % max(1, number_of - fixed)
        return jnp.zeros((number_of,), jnp.int32).at[order[jnp.where(places < fixed, places, moved)]].set(jnp.asarray(tallies, jnp.int32))

    tallies = jnp.where(number % 4 == 0, named(crowded, number // 4), named(usual, number - number // 4 - 1))
    mixed = jax.random.permutation(jax.random.fold_in(own, 3), number_of)
    donor, taker = mixed[0:number_of // 2 * 2:2], mixed[1:number_of // 2 * 2:2]
    room = jnp.minimum(tallies[donor] - 1, limit - tallies[taker]) // 2
    room = jnp.where((donor == order[0]) | (taker == order[0]) | (tallies[taker] == 0), 0, jnp.maximum(room, 0))
    moved = jax.random.randint(jax.random.fold_in(own, 4), (number_of // 2,), 0, 1 << 20) % (room + 1)
    tallies = tallies.at[donor].add(-moved).at[taker].add(moved)
    items = jnp.searchsorted(jnp.cumsum(tallies), jnp.arange(rows * top), side="right").astype(jnp.int32)
    table = items.reshape(top, rows).T
    table = table[jax.random.permutation(jax.random.fold_in(own, 1), rows)]
    offset_by = jax.random.randint(jax.random.fold_in(own, 2), (rows, 1), 0, top)
    return jnp.take_along_axis(table, (jnp.arange(top)[None, :] + offset_by) % top, axis=1)


def load_shares(amount, total, bound, skew, full):
    weights = [(1 << 20) // math.isqrt(rank ** skew) + 1 for rank in range(1, amount + 1)]
    largest = bound if full else min(bound, max(-(-total // amount), total * weights[0] // sum(weights)))
    least = 1 if total - largest >= amount - 1 else 0
    given, spare = [largest] + [least] * (amount - 1), total - largest - least * (amount - 1)
    while spare > 0:
        candidates = [i for i in range(1, amount) if given[i] < largest] or [i for i in range(1, amount) if given[i] < bound]
        pool, budget = sum([weights[i] for i in candidates]), spare
        for i in candidates:
            more = min(bound - given[i], max(1, budget * weights[i] // pool), spare)
            given[i] = given[i] + more
            spare = spare - more
    return np.array(given)


def scatter_about(rng, extent, width, bound, cuts=(), dtype=jnp.bfloat16):
    factor_of = block_scale(rng, extent, cuts, -0.22, 0.18) if cuts else 1.0
    result = jax.random.normal(rng, extent, jnp.float32) * width * factor_of
    return jnp.minimum(jnp.maximum(result, -bound), bound).astype(dtype)


def setup_inputs(seed: int = 0) -> dict:
    seeds = jax.random.split(jax.random.key(seed), 11)
    tokens_in = scatter_about(seeds[0], (TOKENS, D), 1.0, 6.0, ((0, 64), (1, 8)))
    w_kv = scatter_about(seeds[1], (D, KV_HEADS * 2 * HD), D ** -0.5, 0.078125, ((0, 8),))
    queries = draw_queries(jax.random.fold_in(seeds[10], 71), 0)
    k_cache = draw_k_cache(jax.random.fold_in(seeds[10], 71), 0)
    v_cache = scatter_about(seeds[4], (POOL_ALL, KV_HEADS, PAGE, HD), 1.0, 5.0, ((0, 64), (1, 8)))
    page_table = draw_page_table(jax.random.fold_in(seeds[10], 71), 0)
    lengths = draw_lengths(jax.random.fold_in(seeds[10], 71), 0)
    move_dest_keys = jax.random.split(jax.random.fold_in(seeds[7], 1), MOVES // MOVES_DEV)
    move_dest_turns = jax.random.permutation(jax.random.fold_in(seeds[7], 3), MOVES // MOVES_DEV)
    move_dest = jax.vmap(lambda own, number: assign_block(jax.random.fold_in(seeds[7], 2), own, number, MOVES_DEV, N_GEN, 1, CAP, 2))(move_dest_keys, move_dest_turns).reshape((MOVES, 1))
    move_page = with_ends(jax.random.randint(seeds[8], (MOVES,), 0, POOL), jax.random.fold_in(seeds[8], 1), 0, POOL - 1).astype(jnp.int32)
    move_seq = with_ends(jax.random.randint(seeds[9], (MOVES,), 0, SEQ_DEV), jax.random.fold_in(seeds[9], 1), 0, SEQ_DEV - 1).astype(jnp.int32)
    return dict(tokens_in=tokens_in, w_kv=w_kv, queries=queries, k_cache=k_cache, v_cache=v_cache, page_table=page_table, lengths=lengths, move_dest=move_dest, move_page=move_page, move_seq=move_seq)


NEGATIVE = -1e+30

def slot_tables(move_dest, move_page, move_seq, dest_index):
    destinations = move_dest.reshape(N_GEN, MOVES_DEV)
    page_ids = move_page.reshape(N_GEN, MOVES_DEV)
    owner_ids = move_seq.reshape(N_GEN, MOVES_DEV)
    position = jnp.arange(MOVES_DEV)
    earlier = position[None, :] < position[:, None]
    same_dest = destinations[:, :, None] == destinations[:, None, :]
    move_ranks = lax.optimization_barrier(jnp.sum(jnp.where(same_dest & earlier[None], 1, 0), axis=2)).astype(jnp.int32)
    matches = (destinations[:, :, None] == dest_index) & (move_ranks[:, :, None] == jnp.arange(CAP)[None, None, :])
    matches = matches.astype(jnp.int32)
    arrived = lax.optimization_barrier(jnp.sum(matches, axis=1)).reshape(-1).astype(jnp.int32)
    page_at = lax.optimization_barrier(jnp.sum(matches * page_ids[:, :, None], axis=1)).reshape(-1).astype(jnp.int32)
    owner_seq = lax.optimization_barrier(jnp.sum(matches * owner_ids[:, :, None], axis=1)).reshape(-1).astype(jnp.int32)
    return (arrived, page_at, owner_seq)

def to_bf16(values):
    return lax.optimization_barrier(values.astype(jnp.bfloat16)).astype(jnp.float32)

def reference(tokens_in, w_kv, queries, k_cache, v_cache, page_table, lengths, move_dest, move_page, move_seq):
    score_scale = 1.0 / math.sqrt(HD)
    new_kv = jnp.dot(tokens_in, w_kv, preferred_element_type=jnp.float32).astype(jnp.bfloat16)
    fresh_grid = new_kv.reshape(SEQS, STEPS, KV_HEADS, 2, HD)
    query_grid = queries.reshape(SEQS, STEPS, KV_HEADS, GROUP, HD)

    def one_device(dev_index):
        first_seq = (dev_index * SEQ_DEV).astype(jnp.int32)
        query_dev = lax.dynamic_slice_in_dim(query_grid, first_seq, SEQ_DEV, 0).astype(jnp.float32)
        fresh_dev = lax.dynamic_slice_in_dim(fresh_grid, first_seq, SEQ_DEV, 0).astype(jnp.float32)
        page_rows = lax.dynamic_slice_in_dim(page_table, first_seq, SEQ_DEV, 0) + (dev_index * POOL).astype(jnp.int32)
        seq_lengths = lax.dynamic_slice_in_dim(lengths, first_seq, SEQ_DEV, 0)
        arrived, page_at, owner_seq = slot_tables(move_dest, move_page, move_seq, dev_index)
        slot_rows = (jnp.arange(N_GEN * CAP) // CAP).astype(jnp.int32) * POOL + page_at
        slot_keys = k_cache[slot_rows].astype(jnp.float32)
        slot_values = v_cache[slot_rows].astype(jnp.float32)
        slot_query = query_dev[owner_seq]
        slot_scores = jnp.einsum('nicgd,ncpd->nicgp', slot_query, slot_keys) * score_scale
        slot_max = lax.optimization_barrier(jnp.max(slot_scores, axis=-1))
        slot_w = to_bf16(jnp.exp(slot_scores - slot_max[..., None]))
        slot_total = lax.optimization_barrier(jnp.sum(slot_w, axis=-1))
        slot_sum = jnp.einsum('nicgp,ncpd->nicgd', slot_w, slot_values)
        landed = arrived > 0
        slot_max = jnp.where(landed[:, None, None, None], slot_max, NEGATIVE)
        member = (owner_seq[None, :] == jnp.arange(SEQ_DEV)[:, None]) & landed[None, :]
        member_f = member.astype(jnp.float32)
        moved_max = lax.optimization_barrier(jnp.max(jnp.where(member[:, :, None, None, None], slot_max[None], NEGATIVE), axis=1))
        positions = jnp.arange(MAXP * PAGE)
        visible = positions[None, :] < seq_lengths[:, None]
        causal = jnp.arange(STEPS)[None, :] <= jnp.arange(STEPS)[:, None]

        def per_head(head_index):
            query_head = query_dev[:, :, head_index]
            stale_keys = k_cache[page_rows, head_index].astype(jnp.float32).reshape(SEQ_DEV, MAXP * PAGE, HD)
            stale_values = v_cache[page_rows, head_index].astype(jnp.float32).reshape(SEQ_DEV, MAXP * PAGE, HD)
            local_scores = jnp.einsum('sigd,sjd->sigj', query_head, stale_keys) * score_scale
            local_max = lax.optimization_barrier(jnp.max(jnp.where(visible[:, None, None, :], local_scores, NEGATIVE), axis=-1))
            new_keys = fresh_dev[:, :, head_index, 0]
            new_values = fresh_dev[:, :, head_index, 1]
            new_scores = jnp.einsum('sigd,skd->sigk', query_head, new_keys) * score_scale
            new_max = lax.optimization_barrier(jnp.max(jnp.where(causal[None, :, None, :], new_scores, NEGATIVE), axis=-1))
            biggest = jnp.maximum(jnp.maximum(local_max, new_max), moved_max[:, :, head_index])
            local_w = to_bf16(jnp.where(visible[:, None, None, :], jnp.exp(local_scores - biggest[..., None]), 0.0))
            new_w = jnp.where(causal[None, :, None, :], jnp.exp(new_scores - biggest[..., None]), 0.0)
            factor = jnp.exp(slot_max[:, :, head_index] - biggest[owner_seq])
            moved_total = jnp.einsum('sn,nig->sig', member_f, factor * slot_total[:, :, head_index])
            moved_sum = jnp.einsum('sn,nigd->sigd', member_f, factor[..., None] * slot_sum[:, :, head_index])
            numerator = jnp.einsum('sigj,sjd->sigd', local_w, stale_values) + moved_sum + jnp.einsum('sigk,skd->sigd', new_w, new_values)
            denominator = lax.optimization_barrier(jnp.sum(local_w, axis=-1)) + moved_total + lax.optimization_barrier(jnp.sum(new_w, axis=-1))
            return numerator / denominator[..., None]
        by_head = lax.map(per_head, jnp.arange(KV_HEADS))
        return jnp.transpose(by_head, (1, 2, 0, 3, 4))
    every_device = lax.map(one_device, jnp.arange(N_GEN))
    attended = every_device.reshape(SEQS, STEPS, HEADS, HD).astype(jnp.bfloat16)
    return (attended, new_kv)
```

```python
import math

import jax
import jax.numpy as jnp
from jax import lax
from jax.experimental import pallas as pl
from jax.experimental.pallas import tpu as pltpu
from jax.sharding import PartitionSpec as P

GEN = 64
TP = 8
SEQ = 64
ROWS = 10
POOL = 56
PAGE = 64
MAXP = 32
HD = 128
FEAT = 640
TOK = 128
CHUNK = 24
HALF = 12
BLOCK = 128
KEYS = POOL * PAGE
UNIT = 8
NEG = -1e30
SCALE2 = math.log2(math.e) / math.sqrt(HD)

F32 = jnp.float32
BF16 = jnp.bfloat16
I32 = jnp.int32


def iota(shape, dim):
    return lax.broadcasted_iota(I32, shape, dim)


def ones_where(cond):
    return jnp.where(cond, 1.0, 0.0).astype(BF16)


def dot(a, b):
    return jnp.dot(a, b, preferred_element_type=F32)


def dot_t(a, b):
    return lax.dot_general(a, b, (((1,), (1,)), ((), ())), preferred_element_type=F32)


def index_kernel(dest_ref, page_ref, seq_ref, tab_ref):
    me = lax.axis_index("gen")
    dest = dest_ref[...]
    pages = page_ref[...].astype(F32)
    seqs = seq_ref[...].astype(F32)
    src = iota((128, 128), 0)
    dst = iota((128, 128), 1)
    earlier = ones_where((src < dst) & (src // 64 == dst // 64))
    lane = iota((32, 128), 1)
    row = iota((32, 128), 0)

    match = dest == me
    before = dot(ones_where(match), earlier)
    first = match & (before < 0.5)
    second = match & (before > 0.5) & (before < 1.5)
    own = dot(
        jnp.where(first, seqs + 1.0, 0.0).astype(BF16), ones_where(dst == 2 * (src // 64))
    ) + dot(
        jnp.where(second, seqs + 1.0, 0.0).astype(BF16), ones_where(dst == 2 * (src // 64) + 1)
    )
    spread = dot(own.astype(BF16), ones_where((dst % 4 == src) & (src < 4)))
    owner = jnp.sum(jnp.where(lane // 4 == row, spread, 0.0), axis=0, keepdims=True)

    mine = (row == me // 2) & (lane // 64 == me % 2)
    my_dest = jnp.max(jnp.where(mine, dest, -1), axis=0, keepdims=True)
    my_page = jnp.sum(jnp.where(mine, pages, 0.0), axis=0, keepdims=True)
    target = iota((64, 128), 0)
    lane64 = iota((64, 128), 1)
    out = my_dest == target
    before = dot(ones_where(out), earlier)
    first = out & (before < 0.5)
    second = out & (before > 0.5) & (before < 1.5)
    lent = dot(
        jnp.where(first, my_page, 0.0).astype(BF16), ones_where(dst == 0)
    ) + dot(jnp.where(second, my_page, 0.0).astype(BF16), ones_where(dst == 1))
    spread = dot(lent.astype(BF16), ones_where((dst % 2 == src) & (src < 2)))
    lent = jnp.sum(jnp.where(lane64 // 2 == target, spread, 0.0), axis=0, keepdims=True)

    line = iota((8, 128), 0)
    table = jnp.where(
        line == 0,
        jnp.maximum(owner - 1.0, 0.0),
        jnp.where(line == 1, lent, owner - 1.0),
    )
    tab_ref[...] = table.astype(I32)


def main_kernel(
    tab, tab_v, pt_ref, len_ref, x_hbm, w_hbm, k_hbm, v_hbm, q_ref, qs_ref,
    att_ref, kv_ref,
    x_s, w_s, kaug, vaug, qaug, scores, probs, acc, mloc, cnt_s,
    qsend, qrecv, rsend, rrecv, rf, kvsend, kvrecv, nk_s, nv_s,
    load_sem, qs_sem, qr_sem, rs_sem, rr_sem, ks_sem, kr_sem,
):
    me = lax.axis_index("gen")
    me_t = lax.axis_index("tp")

    loads = [
        pltpu.make_async_copy(x_hbm, x_s, load_sem.at[0]),
        pltpu.make_async_copy(w_hbm, w_s, load_sem.at[1]),
        pltpu.make_async_copy(k_hbm, kaug.at[:, :, pl.ds(0, HD)], load_sem.at[2]),
        pltpu.make_async_copy(v_hbm, vaug.at[:, :, pl.ds(0, HD)], load_sem.at[3]),
    ]
    for copy in loads:
        copy.start()

    barrier = pltpu.get_barrier_semaphore()

    @pl.loop(1, GEN)
    def _(off):
        pl.semaphore_signal(
            barrier, inc=1, device_id={"gen": (me + off) % GEN},
            device_id_type=pl.DeviceIdType.MESH,
        )

    @pl.loop(1, TP)
    def _(off):
        pl.semaphore_signal(
            barrier, inc=1, device_id={"tp": (me_t + off) % TP},
            device_id_type=pl.DeviceIdType.MESH,
        )

    @pl.loop(0, GEN // UNIT)
    def _(g):
        for u in range(UNIT):
            n = g * UNIT + u
            qsend[n] = qs_ref[tab[0, 2 * n], 0] + qs_ref[tab[0, 2 * n + 1], 1]

    qrecv[me] = qsend[me]

    pl.semaphore_wait(barrier, GEN - 1 + TP - 1)

    def q_copy(off, peer):
        return pltpu.make_async_remote_copy(
            src_ref=qsend.at[peer], dst_ref=qrecv.at[me],
            send_sem=qs_sem.at[off], recv_sem=qr_sem.at[off],
            device_id={"gen": peer}, device_id_type=pl.DeviceIdType.MESH,
        )

    def r_copy(off, peer):
        return pltpu.make_async_remote_copy(
            src_ref=rsend.at[peer], dst_ref=rrecv.at[me],
            send_sem=rs_sem.at[off], recv_sem=rr_sem.at[off],
            device_id={"gen": peer}, device_id_type=pl.DeviceIdType.MESH,
        )

    def kv_copy(off):
        peer = (me_t + off) % TP
        return pltpu.make_async_remote_copy(
            src_ref=kvsend.at[peer], dst_ref=kvrecv.at[off],
            send_sem=ks_sem.at[off], recv_sem=kr_sem.at[off],
            device_id={"tp": peer}, device_id_type=pl.DeviceIdType.MESH,
        )

    @pl.loop(1, GEN)
    def _(off):
        q_copy(off, (me + off) % GEN).start()

    loads[0].wait()
    loads[1].wait()

    for h in range(TP):
        kvsend[h] = dot(x_s[...], w_s[:, h * 256:(h + 1) * 256])

    table = pt_ref[...].astype(F32).astype(BF16)
    table = jnp.concatenate([table, jnp.zeros((SEQ, MAXP), BF16)], axis=0)
    eye = ones_where(iota((MAXP, MAXP), 0) == iota((MAXP, MAXP), 1))
    table_t = dot_t(eye, table)
    first_row = iota((MAXP, 128), 0).astype(F32) * PAGE
    inside = jnp.clip(len_ref[...].astype(F32) - first_row, 0.0, float(PAGE))
    page = iota((POOL, 128), 0).astype(F32)
    count = jnp.zeros((POOL, 128), F32)
    for m in range(MAXP):
        count = count + jnp.where(table_t[m:m + 1] == page, inside[m:m + 1], 0.0)
    cnt_s[...] = count

    @pl.loop(1, TP)
    def _(off):
        kv_copy(off).start()

    place = iota((PAGE, 128), 0).astype(F32)

    @pl.loop(0, POOL // UNIT)
    def _(g):
        for u in range(UNIT):
            p = g * UNIT + u
            seen = place < cnt_s[pl.ds(p, 1), :]
            kaug[p, :, HD:2 * HD] = jnp.where(seen, 0.0, NEG).astype(BF16)
            vaug[p, :, HD:2 * HD] = jnp.ones((PAGE, HD), BF16)

    member_q = ones_where(iota((SEQ, 128), 0) == iota((SEQ, 128), 1))
    for r in range(ROWS):
        qaug[r * SEQ:(r + 1) * SEQ, 0:HD] = q_ref[r]
        qaug[r * SEQ:(r + 1) * SEQ, HD:2 * HD] = member_q

    loads[2].wait()
    loads[3].wait()

    @pl.loop(0, ROWS * SEQ // BLOCK)
    def _(b):
        rows = pl.ds(pl.multiple_of(b * BLOCK, BLOCK), BLOCK)
        qb = qaug[rows, :]
        top = None
        for c in range(KEYS // 256):
            s = dot_t(qb, kaug[c * 4:(c + 1) * 4].reshape(256, 2 * HD))
            scores[:, c * 256:(c + 1) * 256] = s
            t = jnp.maximum(s[:, :128], s[:, 128:])
            top = t if top is None else jnp.maximum(top, t)
        top = jnp.max(top, axis=1, keepdims=True) * SCALE2
        for c in range(KEYS // 256):
            cols = slice(c * 256, (c + 1) * 256)
            probs[:, cols] = jnp.exp2(scores[:, cols] * SCALE2 - top).astype(BF16)
        acc[rows, :] = dot(probs[...], vaug[...].reshape(KEYS, 2 * HD))
        mloc[rows, :] = jnp.broadcast_to(top, (BLOCK, 128))

    crow = iota((CHUNK, 128), 0)
    clane = iota((CHUNK, 128), 1)
    own_half = crow // HALF == clane // 64
    spot = (clane % 16 == crow % HALF) & (clane < 48) & (crow % HALF < ROWS)

    @pl.loop(0, GEN // UNIT)
    def _(g):
        for u in range(UNIT):
            off = g * UNIT + u

            @pl.when(off > 0)
            def _():
                q_copy(off, (me + GEN - off) % GEN).wait_recv()

        for u in range(UNIT):
            off = g * UNIT + u
            peer = (me + GEN - off) % GEN
            p0 = tab[1, 2 * peer]
            p1 = tab[1, 2 * peer + 1]
            keys = jnp.concatenate([kaug[p0, :, 0:HD], kaug[p1, :, 0:HD]], axis=0)
            vals = jnp.concatenate([vaug[p0], vaug[p1]], axis=0)
            s = jnp.where(own_half, dot_t(qrecv[peer], keys) * SCALE2, NEG)
            top = jnp.max(s, axis=1, keepdims=True)
            o = dot(jnp.exp2(s - top).astype(BF16), vals)
            total = o[:, HD:]
            out = o[:, :HD] / total
            mass = top + jnp.log2(total)
            hi = mass.astype(BF16).astype(F32)
            mid = (mass - hi).astype(BF16).astype(F32)
            low = mass - hi - mid
            parts = jnp.where(clane < 16, hi, jnp.where(clane < 32, mid, low))
            parts = jnp.where(spot, parts, 0.0)
            s0 = jnp.sum(jnp.where(crow < HALF, parts, 0.0), axis=0, keepdims=True)
            s1 = jnp.sum(jnp.where(crow < HALF, 0.0, parts), axis=0, keepdims=True)
            stat = jnp.where(crow < HALF, s0, s1)
            rsend[peer] = jnp.where(crow % HALF == ROWS, stat, out).astype(BF16)

        for u in range(UNIT):
            off = g * UNIT + u

            @pl.when(off > 0)
            def _():
                r_copy(off, (me + GEN - off) % GEN).start()

    rrecv[me] = rsend[me]

    total = kvsend[me_t]
    for off in range(1, TP):
        kv_copy(off).wait_recv()
        total = total + kvrecv[off]
    fresh = total.astype(BF16)
    kv_ref[...] = fresh
    nk_s[...] = fresh[:, :HD].astype(F32)
    nv_s[...] = fresh[:, HD:].astype(F32)

    @pl.loop(0, GEN // UNIT)
    def _(g):
        for u in range(UNIT):
            off = g * UNIT + u

            @pl.when(off > 0)
            def _():
                r_copy(off, (me + off) % GEN).wait_recv()

        for u in range(UNIT):
            peer = (me + g * UNIT + u) % GEN
            rf[pl.ds(pl.multiple_of(peer * CHUNK, 8), CHUNK), :] = rrecv[peer].astype(F32)

    pick = ones_where(
        (iota((16, 128), 1) % 16 == iota((16, 128), 0)) & (iota((16, 128), 1) < 48)
    )
    mass_t = dot_t(pick, rf[pl.ds(ROWS, 2 * GEN, stride=HALF), :].astype(BF16))
    member = tab_v[2:3, :] == iota((SEQ, 128), 0)
    nk = [nk_s[pl.ds(i, SEQ, stride=2), :] for i in range(2)]
    nv = [nv_s[pl.ds(i, SEQ, stride=2), :] for i in range(2)]
    for r in range(ROWS):
        step = r // 5
        rows = slice(r * SEQ, (r + 1) * SEQ)
        q = q_ref[r].astype(F32)
        new = [jnp.sum(q * nk[i], axis=1, keepdims=True) * SCALE2 for i in range(step + 1)]
        moved = jnp.where(member, mass_t[r:r + 1], NEG)
        local = mloc[rows, 0:1]
        big = jnp.maximum(local, jnp.max(moved, axis=1, keepdims=True))
        for s in new:
            big = jnp.maximum(big, s)
        f = jnp.exp2(moved - big)
        part = rf[pl.ds(r, 2 * GEN, stride=HALF), :].astype(BF16)
        f_hi = f.astype(BF16)
        f_low = (f - f_hi.astype(F32)).astype(BF16)
        a = jnp.exp2(local - big)
        num = a * acc[rows, 0:HD] + dot(f_hi, part) + dot(f_low, part)
        den = a * acc[rows, HD:HD + 1] + jnp.sum(f, axis=1, keepdims=True)
        for i, s in enumerate(new):
            e = jnp.exp2(s - big)
            num = num + e * nv[i]
            den = den + e
        att_ref[r] = (num / den).astype(BF16)

    @pl.loop(1, GEN)
    def _(off):
        q_copy(off, (me + off) % GEN).wait_send()
        r_copy(off, (me + GEN - off) % GEN).wait_send()

    @pl.loop(1, TP)
    def _(off):
        kv_copy(off).wait_send()


def per_device(
    tokens_in, w_kv, queries, k_cache, v_cache, page_table, lengths, move_dest, move_page, move_seq
):
    vmem = pl.BlockSpec(memory_space=pltpu.VMEM)
    smem = pl.BlockSpec(memory_space=pltpu.SMEM)
    hbm = pl.BlockSpec(memory_space=pl.ANY)
    tab = pl.pallas_call(
        index_kernel,
        out_shape=jax.ShapeDtypeStruct((8, 128), I32),
        in_specs=[vmem] * 3,
        out_specs=vmem,
        name="index",
    )(move_dest.reshape(32, 128), move_page.reshape(32, 128), move_seq.reshape(32, 128))
    flat = queries.reshape(SEQ, ROWS, HD)
    q_rows = flat.transpose(1, 0, 2)
    q_slots = jnp.stack(
        [jnp.pad(flat, ((0, 0), (0, 14), (0, 0))), jnp.pad(flat, ((0, 0), (12, 2), (0, 0)))],
        axis=1,
    )
    lens = jnp.pad(lengths, (0, 64)).reshape(1, 128)
    dma = pltpu.SemaphoreType.DMA
    att, new_kv = pl.pallas_call(
        main_kernel,
        out_shape=(
            jax.ShapeDtypeStruct((ROWS, SEQ, HD), BF16),
            jax.ShapeDtypeStruct((TOK, 256), BF16),
        ),
        in_specs=[smem, vmem, vmem, vmem, hbm, hbm, hbm, hbm, vmem, vmem],
        out_specs=(vmem, vmem),
        scratch_shapes=[
            pltpu.VMEM((TOK, FEAT), BF16),
            pltpu.VMEM((FEAT, 2048), BF16),
            pltpu.VMEM((POOL, PAGE, 2 * HD), BF16),
            pltpu.VMEM((POOL, PAGE, 2 * HD), BF16),
            pltpu.VMEM((ROWS * SEQ, 2 * HD), BF16),
            pltpu.VMEM((BLOCK, KEYS), F32),
            pltpu.VMEM((BLOCK, KEYS), BF16),
            pltpu.VMEM((ROWS * SEQ, 2 * HD), F32),
            pltpu.VMEM((ROWS * SEQ, 128), F32),
            pltpu.VMEM((POOL, 128), F32),
            pltpu.VMEM((GEN, CHUNK, HD), BF16),
            pltpu.VMEM((GEN, CHUNK, HD), BF16),
            pltpu.VMEM((GEN, CHUNK, HD), BF16),
            pltpu.VMEM((GEN, CHUNK, HD), BF16),
            pltpu.VMEM((GEN * CHUNK, HD), F32),
            pltpu.VMEM((TP, TOK, 256), F32),
            pltpu.VMEM((TP, TOK, 256), F32),
            pltpu.VMEM((TOK, HD), F32),
            pltpu.VMEM((TOK, HD), F32),
            dma((4,)), dma((GEN,)), dma((GEN,)), dma((GEN,)), dma((GEN,)), dma((TP,)), dma((TP,)),
        ],
        compiler_params=pltpu.CompilerParams(
            collective_id=0, has_side_effects=True, vmem_limit_bytes=48 * 1024 * 1024
        ),
        name="decode",
    )(
        tab, tab, page_table, lens, tokens_in, w_kv,
        k_cache.reshape(POOL, PAGE, HD), v_cache.reshape(POOL, PAGE, HD), q_rows, q_slots,
    )
    attended = att.transpose(1, 0, 2).reshape(SEQ, 2, 5, HD)
    return (attended, new_kv)


def solution(mesh):
    return jax.shard_map(
        per_device,
        mesh=mesh,
        in_specs=(
            P("gen", "tp"),
            P("tp", None),
            P("gen", None, "tp", None),
            P("gen", "tp", None, None),
            P("gen", "tp", None, None),
            P("gen", None),
            P("gen"),
            P(),
            P(),
            P(),
        ),
        out_specs=(P("gen", None, "tp", None), P("gen", "tp")),
        check_vma=False,
    )
```

```python
import math

import jax
import jax.numpy as jnp
from jax import lax
from jax.experimental import pallas as pl
from jax.experimental.pallas import tpu as pltpu
from jax.sharding import PartitionSpec as P

GEN = 64
TP = 8
SEQ = 64
ROWS = 10
POOL = 56
PAGE = 64
MAXP = 32
HD = 128
FEAT = 640
TOK = 128
CHUNK = 24
HALF = 12
PART = 320
KEYS = POOL * PAGE
UNIT = 8
WAVE = 16
SUB = 96
STRIDE = 23
NEG = -1e30
SCALE2 = math.log2(math.e) / math.sqrt(HD)

F32 = jnp.float32
BF16 = jnp.bfloat16
I32 = jnp.int32


def turn(step):
    return (step * STRIDE) % GEN


def iota(shape, dim):
    return lax.broadcasted_iota(I32, shape, dim)


def ones_where(cond):
    return jnp.where(cond, 1.0, 0.0).astype(BF16)


def dot(a, b):
    return jnp.dot(a, b, preferred_element_type=F32)


def dot_t(a, b):
    return lax.dot_general(a, b, (((1,), (1,)), ((), ())), preferred_element_type=F32)


def index_kernel(dest_ref, page_ref, seq_ref, tab_ref):
    me = lax.axis_index("gen")
    dest = dest_ref[...]
    pages = page_ref[...].astype(F32)
    seqs = seq_ref[...].astype(F32)
    src = iota((128, 128), 0)
    dst = iota((128, 128), 1)
    earlier = ones_where((src < dst) & (src // 64 == dst // 64))
    lane = iota((32, 128), 1)
    row = iota((32, 128), 0)

    match = dest == me
    before = dot(ones_where(match), earlier)
    first = match & (before < 0.5)
    second = match & (before > 0.5) & (before < 1.5)
    own = dot(
        jnp.where(first, seqs + 1.0, 0.0).astype(BF16), ones_where(dst == 2 * (src // 64))
    ) + dot(
        jnp.where(second, seqs + 1.0, 0.0).astype(BF16), ones_where(dst == 2 * (src // 64) + 1)
    )
    spread = dot(own.astype(BF16), ones_where((dst % 4 == src) & (src < 4)))
    owner = jnp.sum(jnp.where(lane // 4 == row, spread, 0.0), axis=0, keepdims=True)

    mine = (row == me // 2) & (lane // 64 == me % 2)
    my_dest = jnp.max(jnp.where(mine, dest, -1), axis=0, keepdims=True)
    my_page = jnp.sum(jnp.where(mine, pages, 0.0), axis=0, keepdims=True)
    target = iota((64, 128), 0)
    lane64 = iota((64, 128), 1)
    out = my_dest == target
    before = dot(ones_where(out), earlier)
    first = out & (before < 0.5)
    second = out & (before > 0.5) & (before < 1.5)
    lent = dot(
        jnp.where(first, my_page, 0.0).astype(BF16), ones_where(dst == 0)
    ) + dot(jnp.where(second, my_page, 0.0).astype(BF16), ones_where(dst == 1))
    spread = dot(lent.astype(BF16), ones_where((dst % 2 == src) & (src < 2)))
    lent = jnp.sum(jnp.where(lane64 // 2 == target, spread, 0.0), axis=0, keepdims=True)

    line = iota((8, 128), 0)
    table = jnp.where(
        line == 0,
        jnp.maximum(owner - 1.0, 0.0),
        jnp.where(line == 1, lent, owner - 1.0),
    )
    tab_ref[...] = table.astype(I32)


def main_kernel(
    tab, tab_v, pt_ref, len_ref, q_ref, x_hbm, w_hbm, k_hbm, v_hbm,
    att_ref, kv_ref,
    qf, qlow, qhigh, outf, x_s, w_s, kaug, vaug, qaug, scores, probs, top_s,
    acc, mloc, num_s, den_s, cnt_s, sbuf, pbuf, mbuf, obuf,
    qsend, qrecv, rsend, rrecv, rf, kvsend, kvrecv, nk_s, nv_s,
    load_sem, qs_sem, qr_sem, rs_sem, rr_sem, ks_sem, kr_sem,
):
    me = lax.axis_index("gen")
    me_t = lax.axis_index("tp")
    mesh_id = pl.DeviceIdType.MESH

    loads = [
        pltpu.make_async_copy(x_hbm, x_s, load_sem.at[0]),
        pltpu.make_async_copy(w_hbm, w_s, load_sem.at[1]),
        pltpu.make_async_copy(k_hbm, kaug.at[:, :, pl.ds(0, HD)], load_sem.at[2]),
        pltpu.make_async_copy(v_hbm, vaug.at[:, :, pl.ds(0, HD)], load_sem.at[3]),
    ]
    for copy in loads:
        copy.start()

    barrier = pltpu.get_barrier_semaphore()

    def greet(off, carry):
        pl.semaphore_signal(
            barrier, inc=1, device_id={"gen": (me + off) % GEN}, device_id_type=mesh_id
        )
        return carry

    def greet_tp(off, carry):
        pl.semaphore_signal(
            barrier, inc=1, device_id={"tp": (me_t + off) % TP}, device_id_type=mesh_id
        )
        return carry

    lax.fori_loop(1, GEN, greet, 0, unroll=9)
    lax.fori_loop(1, TP, greet_tp, 0, unroll=7)

    qf[...] = q_ref[...].astype(F32)
    member_q = ones_where(iota((SEQ, 128), 0) == iota((SEQ, 128), 1))
    for r in range(HALF):
        if r < ROWS:
            q = qf[pl.ds(r, SEQ, stride=ROWS), :]
            qaug[r * SEQ:(r + 1) * SEQ, 0:HD] = q.astype(BF16)
            qaug[r * SEQ:(r + 1) * SEQ, HD:2 * HD] = member_q
        else:
            q = jnp.zeros((SEQ, HD), F32)
        qlow[:, r, :] = q
        qhigh[:, HALF + r, :] = q

    crow = iota((CHUNK, 128), 0)

    @pl.loop(0, GEN // UNIT)
    def _(g):
        for u in range(UNIT):
            n = g * UNIT + u
            low = qlow[tab[0, 2 * n]]
            high = qhigh[tab[0, 2 * n + 1]]
            qsend[n] = jnp.where(crow < HALF, low, high).astype(BF16)

    qrecv[0] = qsend[me]

    pl.semaphore_wait(barrier, GEN - 1 + TP - 1)

    def q_copy(src, dst, sem, peer):
        return pltpu.make_async_remote_copy(
            src_ref=src, dst_ref=dst, send_sem=qs_sem, recv_sem=qr_sem.at[sem],
            device_id={"gen": peer}, device_id_type=mesh_id,
        )

    def r_copy(src, dst, sem, peer):
        return pltpu.make_async_remote_copy(
            src_ref=src, dst_ref=dst, send_sem=rs_sem, recv_sem=rr_sem.at[sem],
            device_id={"gen": peer}, device_id_type=mesh_id,
        )

    def kv_copy(src, dst, peer):
        return pltpu.make_async_remote_copy(
            src_ref=src, dst_ref=dst, send_sem=ks_sem, recv_sem=kr_sem,
            device_id={"tp": peer}, device_id_type=mesh_id,
        )

    def send_q(step, carry):
        peer = (me + turn(step)) % GEN
        q_copy(qsend.at[peer], qrecv.at[step], step // UNIT, peer).start()
        return carry

    lax.fori_loop(1, GEN, send_q, 0, unroll=9)

    loads[0].wait()
    loads[1].wait()

    for h in range(TP):
        kvsend[h] = dot(x_s[...], w_s[:, h * 256:(h + 1) * 256]).astype(BF16)

    table_t = pt_ref[...].astype(F32)
    table_t = jnp.concatenate([table_t, table_t], axis=1)
    lens = len_ref[...].astype(F32)
    lens = jnp.concatenate([lens, lens], axis=1)
    first_row = iota((MAXP, 128), 0).astype(F32) * PAGE
    inside = jnp.clip(lens - first_row, 0.0, float(PAGE))
    page = iota((POOL, 128), 0).astype(F32)
    count = jnp.zeros((POOL, 128), F32)
    for m in range(MAXP):
        count = count + jnp.where(table_t[m:m + 1] == page, inside[m:m + 1], 0.0)
    cnt_s[...] = count

    def send_kv(off, carry):
        peer = (me_t + off) % TP
        kv_copy(kvsend.at[peer], kvrecv.at[off], peer).start()
        return carry

    lax.fori_loop(1, TP, send_kv, 0, unroll=7)

    place = iota((PAGE, 128), 0).astype(F32)

    @pl.loop(0, POOL // UNIT)
    def _(g):
        for u in range(UNIT):
            p = g * UNIT + u
            seen = place < cnt_s[pl.ds(p, 1), :]
            kaug[p, :, HD:2 * HD] = jnp.where(seen, 0.0, NEG).astype(BF16)
            vaug[p, :, HD:2 * HD] = jnp.ones((PAGE, HD), BF16)

    loads[2].wait()
    loads[3].wait()

    def attend(part):
        rows = slice(part * PART, (part + 1) * PART)
        qb = qaug[rows, :]
        top_s[...] = jnp.full((PART, 128), NEG, F32)

        @pl.loop(0, KEYS // 512)
        def _(c):
            for d in range(2):
                keys = kaug[pl.ds(c * 8 + d * 4, 4)].reshape(256, 2 * HD)
                s = dot_t(qb, keys)
                scores[2 * c + d] = s
                top_s[...] = jnp.maximum(top_s[...], jnp.maximum(s[:, :128], s[:, 128:]))

        top = jnp.max(top_s[...], axis=1, keepdims=True) * SCALE2
        top = jnp.broadcast_to(top, (PART, 128))
        mloc[rows, :] = top

        for c in range(KEYS // 256):
            for d in range(2):
                cols = slice(d * 128, (d + 1) * 128)
                p = jnp.exp2(scores[c, :, cols] * SCALE2 - mloc[rows, :])
                probs[:, c * 256 + d * 128:c * 256 + (d + 1) * 128] = p.astype(BF16)
        acc[rows, :] = dot(probs[...], vaug[...].reshape(KEYS, 2 * HD))

    attend(0)

    srow = iota((SUB, 128), 0) % CHUNK
    slane = iota((SUB, 128), 1)
    own_half = srow // HALF == slane // 64
    spot = (slane % 16 == srow % HALF) & (slane < 48) & (srow % HALF < ROWS)
    gather = ones_where(
        (iota((SUB, SUB), 0) % HALF == ROWS) & (iota((SUB, SUB), 0) // HALF == iota((SUB, SUB), 1) // HALF)
    )

    @pl.loop(0, GEN // WAVE)
    def _(g):
        @pl.when(g == 0)
        def _():
            q_copy(qsend.at[pl.ds(0, 7)], qrecv.at[pl.ds(1, 7)], 0, me).wait_recv()

        @pl.when(g > 0)
        def _():
            q_copy(qsend.at[pl.ds(0, 8)], qrecv.at[pl.ds(g * WAVE, 8)], 2 * g, me).wait_recv()

        q_copy(qsend.at[pl.ds(0, 8)], qrecv.at[pl.ds(g * WAVE + 8, 8)], 2 * g + 1, me).wait_recv()

        pages = []
        for u in range(WAVE):
            step = g * WAVE + u
            peer = (me + GEN - turn(step)) % GEN
            p0 = tab[1, 2 * peer]
            p1 = tab[1, 2 * peer + 1]
            pages.append((p0, p1))
            keys = jnp.concatenate([kaug[p0, :, 0:HD], kaug[p1, :, 0:HD]], axis=0)
            sbuf[u * CHUNK:(u + 1) * CHUNK, :] = dot_t(qrecv[step], keys)
        for b in range(WAVE * CHUNK // SUB):
            rows = slice(b * SUB, (b + 1) * SUB)
            s = jnp.where(own_half, sbuf[rows, :] * SCALE2, NEG)
            top = jnp.broadcast_to(jnp.max(s, axis=1, keepdims=True), (SUB, 128))
            mbuf[rows, :] = top
            pbuf[rows, :] = jnp.exp2(s - top)
        for u in range(WAVE):
            p0, p1 = pages[u]
            vals = jnp.concatenate([vaug[p0], vaug[p1]], axis=0)
            obuf[u * CHUNK:(u + 1) * CHUNK, :] = dot(
                pbuf[u * CHUNK:(u + 1) * CHUNK, :].astype(BF16), vals
            )
        for b in range(WAVE * CHUNK // SUB):
            rows = slice(b * SUB, (b + 1) * SUB)
            total = obuf[rows, HD:]
            out = obuf[rows, :HD] / total
            mass = mbuf[rows, :] + jnp.log2(total)
            hi = mass.astype(BF16).astype(F32)
            mid = (mass - hi).astype(BF16).astype(F32)
            low = mass - hi - mid
            parts = jnp.where(slane < 16, hi, jnp.where(slane < 32, mid, low))
            parts = jnp.where(spot, parts, 0.0).astype(BF16)
            out = jnp.where(srow % HALF == ROWS, dot(gather, parts), out).astype(BF16)
            for j in range(SUB // CHUNK):
                rsend[g * WAVE + b * (SUB // CHUNK) + j] = out[j * CHUNK:(j + 1) * CHUNK]

        for u in range(WAVE):
            step = g * WAVE + u

            def send(step=step):
                peer = (me + GEN - turn(step)) % GEN
                r_copy(rsend.at[step], rrecv.at[step], step // UNIT, peer).start()

            if u == 0:
                pl.when(step > 0)(send)
            else:
                send()

    rrecv[0] = rsend[0]

    attend(1)

    kv_copy(kvsend.at[pl.ds(0, 7)], kvrecv.at[pl.ds(1, 7)], me_t).wait_recv()
    total = kvsend[me_t].astype(F32)
    for off in range(1, TP):
        total = total + kvrecv[off].astype(F32)
    fresh = total.astype(BF16)
    kv_ref[...] = fresh
    nk_s[...] = fresh[:, :HD].astype(F32)
    nv_s[...] = fresh[:, HD:].astype(F32)

    nk = [nk_s[pl.ds(i, SEQ, stride=2), :] for i in range(2)]
    nv = [nv_s[pl.ds(i, SEQ, stride=2), :] for i in range(2)]
    for r in range(ROWS):
        rows = slice(r * SEQ, (r + 1) * SEQ)
        q = qf[pl.ds(r, SEQ, stride=ROWS), :]
        new = [
            jnp.broadcast_to(jnp.sum(q * nk[i], axis=1, keepdims=True) * SCALE2, (SEQ, 128))
            for i in range(r % 2 + 1)
        ]
        local = mloc[rows, :]
        big = local
        for s in new:
            big = jnp.maximum(big, s)
        a = jnp.exp2(local - big)
        num = a * acc[rows, 0:HD]
        den = a * acc[rows, HD:2 * HD]
        for i, s in enumerate(new):
            e = jnp.exp2(s - big)
            num = num + e * nv[i]
            den = den + e
        mloc[rows, :] = big
        num_s[rows, :] = num
        den_s[rows, :] = den

    @pl.loop(0, GEN // UNIT)
    def _(g):
        @pl.when(g == 0)
        def _():
            r_copy(rsend.at[pl.ds(0, 7)], rrecv.at[pl.ds(1, 7)], 0, me).wait_recv()

        @pl.when(g > 0)
        def _():
            r_copy(rsend.at[pl.ds(0, 8)], rrecv.at[pl.ds(g * UNIT, 8)], g, me).wait_recv()

        for u in range(UNIT):
            step = g * UNIT + u
            peer = (me + turn(step)) % GEN
            rf[pl.ds(pl.multiple_of(peer * CHUNK, 8), CHUNK), :] = rrecv[step].astype(F32)

    pick = ones_where(
        (iota((16, 128), 1) % 16 == iota((16, 128), 0)) & (iota((16, 128), 1) < 48)
    )
    mass_t = dot_t(pick, rf[pl.ds(ROWS, 2 * GEN, stride=HALF), :].astype(BF16))
    member = tab_v[2:3, :] == iota((SEQ, 128), 0)
    ones = jnp.ones((2 * GEN, HD), BF16)
    for r in range(ROWS):
        rows = slice(r * SEQ, (r + 1) * SEQ)
        moved = jnp.where(member, mass_t[r:r + 1], NEG)
        before = mloc[rows, :]
        big = jnp.maximum(before, jnp.max(moved, axis=1, keepdims=True))
        f = jnp.exp2(moved - big)
        part = rf[pl.ds(r, 2 * GEN, stride=HALF), :].astype(BF16)
        part = jnp.concatenate([part, ones], axis=1)
        f_hi = f.astype(BF16)
        f_low = (f - f_hi.astype(F32)).astype(BF16)
        a = jnp.exp2(before - big)
        extra = dot(f_hi, part) + dot(f_low, part)
        num = a * num_s[rows, :] + extra[:, :HD]
        den = a * den_s[rows, :] + extra[:, HD:]
        outf[pl.ds(r, SEQ, stride=ROWS), :] = num / den

    att_ref[...] = outf[...].astype(BF16)

    q_copy(qsend.at[pl.ds(0, GEN - 1)], qrecv.at[pl.ds(0, GEN - 1)], 0, me).wait_send()
    r_copy(rsend.at[pl.ds(0, GEN - 1)], rrecv.at[pl.ds(0, GEN - 1)], 0, me).wait_send()
    kv_copy(kvsend.at[pl.ds(0, TP - 1)], kvrecv.at[pl.ds(0, TP - 1)], me_t).wait_send()


def copy_kernel(att_in, kv_in, att_out, kv_out, att_s, kv_s, sem):
    first = [
        pltpu.make_async_copy(att_in, att_s, sem.at[0]),
        pltpu.make_async_copy(kv_in, kv_s, sem.at[1]),
    ]
    second = [
        pltpu.make_async_copy(att_s, att_out, sem.at[2]),
        pltpu.make_async_copy(kv_s, kv_out, sem.at[3]),
    ]
    for copy in first:
        copy.start()
    for copy, onward in zip(first, second):
        copy.wait()
        onward.start()
    for copy in second:
        copy.wait()


def per_device(
    tokens_in, w_kv, queries, k_cache, v_cache, page_table, lengths, move_dest, move_page, move_seq
):
    vmem = pl.BlockSpec(memory_space=pltpu.VMEM)
    smem = pl.BlockSpec(memory_space=pltpu.SMEM)
    hbm = pl.BlockSpec(memory_space=pltpu.HBM)
    tab = pl.pallas_call(
        index_kernel,
        out_shape=jax.ShapeDtypeStruct((8, 128), I32),
        in_specs=[vmem] * 3,
        out_specs=vmem,
        name="index",
    )(move_dest.reshape(32, 128), move_page.reshape(32, 128), move_seq.reshape(32, 128))
    dma = pltpu.SemaphoreType.DMA
    att, new_kv = pl.pallas_call(
        main_kernel,
        out_shape=(
            jax.ShapeDtypeStruct((SEQ * ROWS, HD), BF16),
            jax.ShapeDtypeStruct((TOK, 256), BF16),
        ),
        in_specs=[smem] + [vmem] * 4 + [hbm] * 4,
        out_specs=(vmem, vmem),
        scratch_shapes=[
            pltpu.VMEM((SEQ * ROWS, HD), F32),
            pltpu.VMEM((SEQ, CHUNK, HD), F32),
            pltpu.VMEM((SEQ, CHUNK, HD), F32),
            pltpu.VMEM((SEQ * ROWS, HD), F32),
            pltpu.VMEM((TOK, FEAT), BF16),
            pltpu.VMEM((FEAT, 2048), BF16),
            pltpu.VMEM((POOL, PAGE, 2 * HD), BF16),
            pltpu.VMEM((POOL, PAGE, 2 * HD), BF16),
            pltpu.VMEM((ROWS * SEQ, 2 * HD), BF16),
            pltpu.VMEM((KEYS // 256, PART, 256), F32),
            pltpu.VMEM((PART, KEYS), BF16),
            pltpu.VMEM((PART, 128), F32),
            pltpu.VMEM((ROWS * SEQ, 2 * HD), F32),
            pltpu.VMEM((ROWS * SEQ, 128), F32),
            pltpu.VMEM((ROWS * SEQ, 128), F32),
            pltpu.VMEM((ROWS * SEQ, 128), F32),
            pltpu.VMEM((POOL, 128), F32),
            pltpu.VMEM((WAVE * CHUNK, 128), F32),
            pltpu.VMEM((WAVE * CHUNK, 128), F32),
            pltpu.VMEM((WAVE * CHUNK, 128), F32),
            pltpu.VMEM((WAVE * CHUNK, 2 * HD), F32),
            pltpu.VMEM((GEN, CHUNK, HD), BF16),
            pltpu.VMEM((GEN, CHUNK, HD), BF16),
            pltpu.VMEM((GEN, CHUNK, HD), BF16),
            pltpu.VMEM((GEN, CHUNK, HD), BF16),
            pltpu.VMEM((GEN * CHUNK, HD), F32),
            pltpu.VMEM((TP, TOK, 256), BF16),
            pltpu.VMEM((TP, TOK, 256), BF16),
            pltpu.VMEM((TOK, HD), F32),
            pltpu.VMEM((TOK, HD), F32),
            dma((4,)), dma(()), dma((GEN // UNIT,)), dma(()), dma((GEN // UNIT,)), dma(()), dma(()),
        ],
        compiler_params=pltpu.CompilerParams(
            collective_id=0, has_side_effects=True, vmem_limit_bytes=67043328
        ),
        name="decode",
    )(
        tab, tab, page_table.T, lengths.reshape(1, SEQ),
        queries.transpose(0, 2, 1, 3).reshape(SEQ * ROWS, HD), tokens_in, w_kv,
        k_cache.reshape(POOL, PAGE, HD), v_cache.reshape(POOL, PAGE, HD),
    )
    shapes = (
        jax.ShapeDtypeStruct((SEQ * ROWS, HD), BF16),
        jax.ShapeDtypeStruct((TOK, 256), BF16),
    )
    att, new_kv = pl.pallas_call(
        copy_kernel,
        out_shape=shapes,
        in_specs=[hbm] * 2,
        out_specs=(hbm, hbm),
        scratch_shapes=[
            pltpu.VMEM((SEQ * ROWS, HD), BF16), pltpu.VMEM((TOK, 256), BF16), dma((4,)),
        ],
        compiler_params=pltpu.CompilerParams(vmem_limit_bytes=67043328),
        name="deliver",
    )(att, new_kv)
    attended = att.reshape(SEQ, 5, 2, HD).transpose(0, 2, 1, 3)
    return (attended, new_kv)


def solution(mesh):
    return jax.shard_map(
        per_device,
        mesh=mesh,
        in_specs=(
            P("gen", "tp"),
            P("tp", None),
            P("gen", None, "tp", None),
            P("gen", "tp", None, None),
            P("gen", "tp", None, None),
            P("gen", None),
            P("gen"),
            P(),
            P(),
            P(),
        ),
        out_specs=(P("gen", None, "tp", None), P("gen", "tp")),
        check_vma=False,
    )
```

```python
import math

import jax
import jax.numpy as jnp
from jax import lax
from jax.experimental import pallas as pl
from jax.experimental.pallas import tpu as pltpu
from jax.sharding import PartitionSpec as P

GEN = 64
TP = 8
SEQ = 64
ROWS = 10
POOL = 56
PAGE = 64
MAXP = 32
HD = 128
FEAT = 640
TOK = 128
CHUNK = 24
HALF = 12
PART = 320
KEYS = POOL * PAGE
UNIT = 8
WAVE = 16
SUB = 96
STRIDE = 23
NEG = -1e30
SCALE2 = math.log2(math.e) / math.sqrt(HD)

F32 = jnp.float32
BF16 = jnp.bfloat16
I32 = jnp.int32


def turn(step):
    return (step * STRIDE) % GEN


def iota(shape, dim):
    return lax.broadcasted_iota(I32, shape, dim)


def ones_where(cond):
    return jnp.where(cond, 1.0, 0.0).astype(BF16)


def dot(a, b):
    return jnp.dot(a, b, preferred_element_type=F32)


def dot_t(a, b):
    return lax.dot_general(a, b, (((1,), (1,)), ((), ())), preferred_element_type=F32)


def running(x, width):
    lane = iota(x.shape, 1) % width
    reach = 1
    while reach < width:
        x = x + jnp.where(lane >= reach, pltpu.roll(x, reach, 1), 0)
        reach *= 2
    return x


def first_two(match, values, width):
    hit = jnp.where(match, 1, 0)
    before = running(hit, width) - hit
    first = running(jnp.where(match & (before == 0), values, 0), width)
    second = running(jnp.where(match & (before == 1), values, 0), width)
    return first, second


def slot_owner(me, dest, seqs):
    src = iota((128, 128), 0)
    dst = iota((128, 128), 1)
    earlier = ones_where((src < dst) & (src // 64 == dst // 64))
    lane = iota((32, 128), 1)
    row = iota((32, 128), 0)
    match = dest == me
    before = dot(ones_where(match), earlier)
    first = match & (before < 0.5)
    second = match & (before > 0.5) & (before < 1.5)
    seqs = seqs.astype(F32) + 1.0
    own = dot(
        jnp.where(first, seqs, 0.0).astype(BF16), ones_where(dst == 2 * (src // 64))
    ) + dot(
        jnp.where(second, seqs, 0.0).astype(BF16), ones_where(dst == 2 * (src // 64) + 1)
    )
    spread = dot(own.astype(BF16), ones_where((dst % 4 == src) & (src < 4)))
    return jnp.sum(jnp.where(lane // 4 == row, spread, 0.0), axis=0, keepdims=True) - 1.0


def main_kernel(
    dest_ref, page_ref, seq_ref, pt_ref, len_ref, q_ref, x_hbm, w_hbm, k_hbm, v_hbm,
    att_ref, kv_ref,
    owner_s, own_s, own_v, lent_s, lent_v, qf, qlow, qhigh, outf, x_s, w_s, kaug, vaug, qaug, scores, probs, top_s,
    acc, mloc, num_s, den_s, cnt_s, sbuf, pbuf, mbuf, obuf,
    qsend, qrecv, rsend, rrecv, rf, kvsend, kvrecv, nk_s, nv_s,
    load_sem, tab_sem, qs_sem, qr_sem, rs_sem, rr_sem, ks_sem, kr_sem,
):
    me = lax.axis_index("gen")
    me_t = lax.axis_index("tp")
    mesh_id = pl.DeviceIdType.MESH

    loads = [
        pltpu.make_async_copy(x_hbm, x_s, load_sem.at[0]),
        pltpu.make_async_copy(w_hbm, w_s, load_sem.at[1]),
        pltpu.make_async_copy(k_hbm, kaug.at[:, :, pl.ds(0, HD)], load_sem.at[2]),
        pltpu.make_async_copy(v_hbm, vaug.at[:, :, pl.ds(0, HD)], load_sem.at[3]),
    ]
    for copy in loads:
        copy.start()

    barrier = pltpu.get_barrier_semaphore()

    def greet(off, carry):
        pl.semaphore_signal(
            barrier, inc=1, device_id={"gen": (me + off) % GEN}, device_id_type=mesh_id
        )
        return carry

    def greet_tp(off, carry):
        pl.semaphore_signal(
            barrier, inc=1, device_id={"tp": (me_t + off) % TP}, device_id_type=mesh_id
        )
        return carry

    lax.fori_loop(1, GEN, greet, 0, unroll=9)
    lax.fori_loop(1, TP, greet_tp, 0, unroll=7)

    dest = dest_ref[...]
    own_v[0], own_v[1] = first_two(dest == me, seq_ref[...], 64)
    row = iota((32, 128), 0)
    mine = (row == me // 2) & (iota((32, 128), 1) // 64 == me % 2)
    my_dest = jnp.max(jnp.where(mine, dest, -1), axis=0, keepdims=True)
    my_page = jnp.max(jnp.where(mine, page_ref[...], 0), axis=0, keepdims=True)
    to_own = pltpu.make_async_copy(own_v, own_s, tab_sem.at[0])
    to_own.start()
    target = iota((GEN, 128), 0)
    my_page = jnp.broadcast_to(my_page, (GEN, 128))
    lent_v[0], lent_v[1] = first_two(my_dest == target, my_page, 128)
    to_lent = pltpu.make_async_copy(lent_v, lent_s, tab_sem.at[1])
    to_lent.start()

    qf[...] = q_ref[...].astype(F32)
    member_q = ones_where(iota((SEQ, 128), 0) == iota((SEQ, 128), 1))
    for r in range(HALF):
        if r < ROWS:
            q = qf[pl.ds(r, SEQ, stride=ROWS), :]
            qaug[r * SEQ:(r + 1) * SEQ, 0:HD] = q.astype(BF16)
            qaug[r * SEQ:(r + 1) * SEQ, HD:2 * HD] = member_q
        else:
            q = jnp.zeros((SEQ, HD), F32)
        qlow[:, r, :] = q
        qhigh[:, HALF + r, :] = q

    to_own.wait()

    crow = iota((CHUNK, 128), 0)

    @pl.loop(0, GEN // UNIT)
    def _(g):
        for u in range(UNIT):
            n = g * UNIT + u
            low = qlow[own_s[0, n // 2, n % 2 * 64 + 63]]
            high = qhigh[own_s[1, n // 2, n % 2 * 64 + 63]]
            qsend[n] = jnp.where(crow < HALF, low, high).astype(BF16)

    qrecv[0] = qsend[me]

    pl.semaphore_wait(barrier, GEN - 1 + TP - 1)

    def q_copy(src, dst, sem, peer):
        return pltpu.make_async_remote_copy(
            src_ref=src, dst_ref=dst, send_sem=qs_sem, recv_sem=qr_sem.at[sem],
            device_id={"gen": peer}, device_id_type=mesh_id,
        )

    def r_copy(src, dst, sem, peer):
        return pltpu.make_async_remote_copy(
            src_ref=src, dst_ref=dst, send_sem=rs_sem, recv_sem=rr_sem.at[sem],
            device_id={"gen": peer}, device_id_type=mesh_id,
        )

    def kv_copy(src, dst, peer):
        return pltpu.make_async_remote_copy(
            src_ref=src, dst_ref=dst, send_sem=ks_sem, recv_sem=kr_sem,
            device_id={"tp": peer}, device_id_type=mesh_id,
        )

    def send_q(step, carry):
        peer = (me + turn(step)) % GEN
        q_copy(qsend.at[peer], qrecv.at[step], step // UNIT, peer).start()
        return carry

    lax.fori_loop(1, GEN, send_q, 0, unroll=9)

    loads[0].wait()
    loads[1].wait()

    for h in range(TP):
        kvsend[h] = dot(x_s[...], w_s[:, h * 256:(h + 1) * 256]).astype(BF16)

    table_t = pt_ref[...].astype(F32)
    table_t = jnp.concatenate([table_t, table_t], axis=1)
    lens = len_ref[...].astype(F32)
    lens = jnp.concatenate([lens, lens], axis=1)
    first_row = iota((MAXP, 128), 0).astype(F32) * PAGE
    inside = jnp.clip(lens - first_row, 0.0, float(PAGE))
    page = iota((POOL, 128), 0).astype(F32)
    count = jnp.zeros((POOL, 128), F32)
    for m in range(MAXP):
        count = count + jnp.where(table_t[m:m + 1] == page, inside[m:m + 1], 0.0)
    cnt_s[...] = count

    def send_kv(off, carry):
        peer = (me_t + off) % TP
        kv_copy(kvsend.at[peer], kvrecv.at[off], peer).start()
        return carry

    lax.fori_loop(1, TP, send_kv, 0, unroll=7)

    place = iota((PAGE, 128), 0).astype(F32)

    @pl.loop(0, POOL // UNIT)
    def _(g):
        for u in range(UNIT):
            p = g * UNIT + u
            seen = place < cnt_s[pl.ds(p, 1), :]
            kaug[p, :, HD:2 * HD] = jnp.where(seen, 0.0, NEG).astype(BF16)
            vaug[p, :, HD:2 * HD] = jnp.ones((PAGE, HD), BF16)

    loads[2].wait()
    loads[3].wait()

    def attend(part):
        rows = slice(part * PART, (part + 1) * PART)
        qb = qaug[rows, :]
        top_s[...] = jnp.full((PART, 128), NEG, F32)

        @pl.loop(0, KEYS // 512)
        def _(c):
            for d in range(2):
                keys = kaug[pl.ds(c * 8 + d * 4, 4)].reshape(256, 2 * HD)
                s = dot_t(qb, keys)
                scores[2 * c + d] = s
                top_s[...] = jnp.maximum(top_s[...], jnp.maximum(s[:, :128], s[:, 128:]))

        top = jnp.max(top_s[...], axis=1, keepdims=True) * SCALE2
        top = jnp.broadcast_to(top, (PART, 128))
        mloc[rows, :] = top

        for c in range(KEYS // 256):
            for d in range(2):
                cols = slice(d * 128, (d + 1) * 128)
                p = jnp.exp2(scores[c, :, cols] * SCALE2 - mloc[rows, :])
                probs[:, c * 256 + d * 128:c * 256 + (d + 1) * 128] = p.astype(BF16)
        acc[rows, :] = dot(probs[...], vaug[...].reshape(KEYS, 2 * HD))

    attend(0)

    to_lent.wait()

    srow = iota((SUB, 128), 0) % CHUNK
    slane = iota((SUB, 128), 1)
    own_half = srow // HALF == slane // 64
    spot = (slane % 16 == srow % HALF) & (slane < 48) & (srow % HALF < ROWS)
    gather = ones_where(
        (iota((SUB, SUB), 0) % HALF == ROWS) & (iota((SUB, SUB), 0) // HALF == iota((SUB, SUB), 1) // HALF)
    )

    @pl.loop(0, GEN // WAVE)
    def _(g):
        @pl.when(g == 0)
        def _():
            q_copy(qsend.at[pl.ds(0, 7)], qrecv.at[pl.ds(1, 7)], 0, me).wait_recv()

        @pl.when(g > 0)
        def _():
            q_copy(qsend.at[pl.ds(0, 8)], qrecv.at[pl.ds(g * WAVE, 8)], 2 * g, me).wait_recv()

        q_copy(qsend.at[pl.ds(0, 8)], qrecv.at[pl.ds(g * WAVE + 8, 8)], 2 * g + 1, me).wait_recv()

        pages = []
        for u in range(WAVE):
            step = g * WAVE + u
            peer = (me + GEN - turn(step)) % GEN
            p0 = lent_s[0, peer, 127]
            p1 = lent_s[1, peer, 127]
            pages.append((p0, p1))
            keys = jnp.concatenate([kaug[p0, :, 0:HD], kaug[p1, :, 0:HD]], axis=0)
            sbuf[u * CHUNK:(u + 1) * CHUNK, :] = dot_t(qrecv[step], keys)
        for b in range(WAVE * CHUNK // SUB):
            rows = slice(b * SUB, (b + 1) * SUB)
            s = jnp.where(own_half, sbuf[rows, :] * SCALE2, NEG)
            top = jnp.broadcast_to(jnp.max(s, axis=1, keepdims=True), (SUB, 128))
            mbuf[rows, :] = top
            pbuf[rows, :] = jnp.exp2(s - top)
        for u in range(WAVE):
            p0, p1 = pages[u]
            vals = jnp.concatenate([vaug[p0], vaug[p1]], axis=0)
            obuf[u * CHUNK:(u + 1) * CHUNK, :] = dot(
                pbuf[u * CHUNK:(u + 1) * CHUNK, :].astype(BF16), vals
            )
        for b in range(WAVE * CHUNK // SUB):
            rows = slice(b * SUB, (b + 1) * SUB)
            total = obuf[rows, HD:]
            out = obuf[rows, :HD] / total
            mass = mbuf[rows, :] + jnp.log2(total)
            hi = mass.astype(BF16).astype(F32)
            mid = (mass - hi).astype(BF16).astype(F32)
            low = mass - hi - mid
            parts = jnp.where(slane < 16, hi, jnp.where(slane < 32, mid, low))
            parts = jnp.where(spot, parts, 0.0).astype(BF16)
            out = jnp.where(srow % HALF == ROWS, dot(gather, parts), out).astype(BF16)
            for j in range(SUB // CHUNK):
                rsend[g * WAVE + b * (SUB // CHUNK) + j] = out[j * CHUNK:(j + 1) * CHUNK]

        for u in range(WAVE):
            step = g * WAVE + u

            def send(step=step):
                peer = (me + GEN - turn(step)) % GEN
                r_copy(rsend.at[step], rrecv.at[step], step // UNIT, peer).start()

            if u == 0:
                pl.when(step > 0)(send)
            else:
                send()

    rrecv[0] = rsend[0]

    attend(1)
    owner_s[...] = slot_owner(me, dest_ref[...], seq_ref[...])

    kv_copy(kvsend.at[pl.ds(0, 7)], kvrecv.at[pl.ds(1, 7)], me_t).wait_recv()
    total = kvsend[me_t].astype(F32)
    for off in range(1, TP):
        total = total + kvrecv[off].astype(F32)
    fresh = total.astype(BF16)
    kv_ref[...] = fresh
    nk_s[...] = fresh[:, :HD].astype(F32)
    nv_s[...] = fresh[:, HD:].astype(F32)

    nk = [nk_s[pl.ds(i, SEQ, stride=2), :] for i in range(2)]
    nv = [nv_s[pl.ds(i, SEQ, stride=2), :] for i in range(2)]
    for r in range(ROWS):
        rows = slice(r * SEQ, (r + 1) * SEQ)
        q = qf[pl.ds(r, SEQ, stride=ROWS), :]
        new = [
            jnp.broadcast_to(jnp.sum(q * nk[i], axis=1, keepdims=True) * SCALE2, (SEQ, 128))
            for i in range(r % 2 + 1)
        ]
        local = mloc[rows, :]
        big = local
        for s in new:
            big = jnp.maximum(big, s)
        a = jnp.exp2(local - big)
        num = a * acc[rows, 0:HD]
        den = a * acc[rows, HD:2 * HD]
        for i, s in enumerate(new):
            e = jnp.exp2(s - big)
            num = num + e * nv[i]
            den = den + e
        mloc[rows, :] = big
        num_s[rows, :] = num
        den_s[rows, :] = den

    @pl.loop(0, GEN // UNIT)
    def _(g):
        @pl.when(g == 0)
        def _():
            r_copy(rsend.at[pl.ds(0, 7)], rrecv.at[pl.ds(1, 7)], 0, me).wait_recv()

        @pl.when(g > 0)
        def _():
            r_copy(rsend.at[pl.ds(0, 8)], rrecv.at[pl.ds(g * UNIT, 8)], g, me).wait_recv()

        for u in range(UNIT):
            step = g * UNIT + u
            peer = (me + turn(step)) % GEN
            rf[pl.ds(pl.multiple_of(peer * CHUNK, 8), CHUNK), :] = rrecv[step].astype(F32)

    pick = ones_where(
        (iota((16, 128), 1) % 16 == iota((16, 128), 0)) & (iota((16, 128), 1) < 48)
    )
    mass_t = dot_t(pick, rf[pl.ds(ROWS, 2 * GEN, stride=HALF), :].astype(BF16))
    member = owner_s[...] == iota((SEQ, 128), 0).astype(F32)
    ones = jnp.ones((2 * GEN, HD), BF16)
    for r in range(ROWS):
        rows = slice(r * SEQ, (r + 1) * SEQ)
        moved = jnp.where(member, mass_t[r:r + 1], NEG)
        before = mloc[rows, :]
        big = jnp.maximum(before, jnp.max(moved, axis=1, keepdims=True))
        f = jnp.exp2(moved - big)
        part = rf[pl.ds(r, 2 * GEN, stride=HALF), :].astype(BF16)
        part = jnp.concatenate([part, ones], axis=1)
        f_hi = f.astype(BF16)
        f_low = (f - f_hi.astype(F32)).astype(BF16)
        a = jnp.exp2(before - big)
        extra = dot(f_hi, part) + dot(f_low, part)
        num = a * num_s[rows, :] + extra[:, :HD]
        den = a * den_s[rows, :] + extra[:, HD:]
        outf[pl.ds(r, SEQ, stride=ROWS), :] = num / den

    att_ref[...] = outf[...].astype(BF16)

    q_copy(qsend.at[pl.ds(0, GEN - 1)], qrecv.at[pl.ds(0, GEN - 1)], 0, me).wait_send()
    r_copy(rsend.at[pl.ds(0, GEN - 1)], rrecv.at[pl.ds(0, GEN - 1)], 0, me).wait_send()
    kv_copy(kvsend.at[pl.ds(0, TP - 1)], kvrecv.at[pl.ds(0, TP - 1)], me_t).wait_send()


def copy_kernel(att_in, kv_in, att_out, kv_out, att_s, kv_s, sem):
    first = [
        pltpu.make_async_copy(att_in, att_s, sem.at[0]),
        pltpu.make_async_copy(kv_in, kv_s, sem.at[1]),
    ]
    second = [
        pltpu.make_async_copy(att_s, att_out, sem.at[2]),
        pltpu.make_async_copy(kv_s, kv_out, sem.at[3]),
    ]
    for copy in first:
        copy.start()
    for copy, onward in zip(first, second):
        copy.wait()
        onward.start()
    for copy in second:
        copy.wait()


def per_device(
    tokens_in, w_kv, queries, k_cache, v_cache, page_table, lengths, move_dest, move_page, move_seq
):
    vmem = pl.BlockSpec(memory_space=pltpu.VMEM)
    hbm = pl.BlockSpec(memory_space=pltpu.HBM)
    dma = pltpu.SemaphoreType.DMA
    att, new_kv = pl.pallas_call(
        main_kernel,
        out_shape=(
            jax.ShapeDtypeStruct((SEQ * ROWS, HD), BF16),
            jax.ShapeDtypeStruct((TOK, 256), BF16),
        ),
        in_specs=[vmem] * 6 + [hbm] * 4,
        out_specs=(vmem, vmem),
        scratch_shapes=[
            pltpu.VMEM((1, 128), F32),
            pltpu.SMEM((2, 32, 128), I32),
            pltpu.VMEM((2, 32, 128), I32),
            pltpu.SMEM((2, GEN, 128), I32),
            pltpu.VMEM((2, GEN, 128), I32),
            pltpu.VMEM((SEQ * ROWS, HD), F32),
            pltpu.VMEM((SEQ, CHUNK, HD), F32),
            pltpu.VMEM((SEQ, CHUNK, HD), F32),
            pltpu.VMEM((SEQ * ROWS, HD), F32),
            pltpu.VMEM((TOK, FEAT), BF16),
            pltpu.VMEM((FEAT, 2048), BF16),
            pltpu.VMEM((POOL, PAGE, 2 * HD), BF16),
            pltpu.VMEM((POOL, PAGE, 2 * HD), BF16),
            pltpu.VMEM((ROWS * SEQ, 2 * HD), BF16),
            pltpu.VMEM((KEYS // 256, PART, 256), F32),
            pltpu.VMEM((PART, KEYS), BF16),
            pltpu.VMEM((PART, 128), F32),
            pltpu.VMEM((ROWS * SEQ, 2 * HD), F32),
            pltpu.VMEM((ROWS * SEQ, 128), F32),
            pltpu.VMEM((ROWS * SEQ, 128), F32),
            pltpu.VMEM((ROWS * SEQ, 128), F32),
            pltpu.VMEM((POOL, 128), F32),
            pltpu.VMEM((WAVE * CHUNK, 128), F32),
            pltpu.VMEM((WAVE * CHUNK, 128), F32),
            pltpu.VMEM((WAVE * CHUNK, 128), F32),
            pltpu.VMEM((WAVE * CHUNK, 2 * HD), F32),
            pltpu.VMEM((GEN, CHUNK, HD), BF16),
            pltpu.VMEM((GEN, CHUNK, HD), BF16),
            pltpu.VMEM((GEN, CHUNK, HD), BF16),
            pltpu.VMEM((GEN, CHUNK, HD), BF16),
            pltpu.VMEM((GEN * CHUNK, HD), F32),
            pltpu.VMEM((TP, TOK, 256), BF16),
            pltpu.VMEM((TP, TOK, 256), BF16),
            pltpu.VMEM((TOK, HD), F32),
            pltpu.VMEM((TOK, HD), F32),
            dma((4,)), dma((2,)), dma(()), dma((GEN // UNIT,)), dma(()), dma((GEN // UNIT,)), dma(()), dma(()),
        ],
        compiler_params=pltpu.CompilerParams(
            collective_id=0, has_side_effects=True, vmem_limit_bytes=67043328
        ),
        name="decode",
    )(
        move_dest.reshape(32, 128), move_page.reshape(32, 128), move_seq.reshape(32, 128),
        page_table.T, lengths.reshape(1, SEQ),
        queries.transpose(0, 2, 1, 3).reshape(SEQ * ROWS, HD), tokens_in, w_kv,
        k_cache.reshape(POOL, PAGE, HD), v_cache.reshape(POOL, PAGE, HD),
    )
    shapes = (
        jax.ShapeDtypeStruct((SEQ * ROWS, HD), BF16),
        jax.ShapeDtypeStruct((TOK, 256), BF16),
    )
    att, new_kv = pl.pallas_call(
        copy_kernel,
        out_shape=shapes,
        in_specs=[hbm] * 2,
        out_specs=(hbm, hbm),
        scratch_shapes=[
            pltpu.VMEM((SEQ * ROWS, HD), BF16), pltpu.VMEM((TOK, 256), BF16), dma((4,)),
        ],
        compiler_params=pltpu.CompilerParams(vmem_limit_bytes=67043328),
        name="deliver",
    )(att, new_kv)
    attended = att.reshape(SEQ, 5, 2, HD).transpose(0, 2, 1, 3)
    return (attended, new_kv)


def solution(mesh):
    return jax.shard_map(
        per_device,
        mesh=mesh,
        in_specs=(
            P("gen", "tp"),
            P("tp", None),
            P("gen", None, "tp", None),
            P("gen", "tp", None, None),
            P("gen", "tp", None, None),
            P("gen", None),
            P("gen"),
            P(),
            P(),
            P(),
        ),
        out_specs=(P("gen", None, "tp", None), P("gen", "tp")),
        check_vma=False,
    )
```

```python
import math

import jax
import jax.numpy as jnp
from jax import lax
from jax.experimental import pallas as pl
from jax.experimental.pallas import tpu as pltpu
from jax.sharding import PartitionSpec as P

GEN = 64
TP = 8
SEQ = 64
ROWS = 10
POOL = 56
PAGE = 64
MAXP = 32
HD = 128
FEAT = 640
TOK = 128
CHUNK = 24
HALF = 12
PART = 320
KEYS = POOL * PAGE
UNIT = 8
WAVE = 16
SUB = 96
PLANE = 16
PLANES = GEN // PLANE
STRIDE = 23
NEG = -1e30
SCALE2 = math.log2(math.e) / math.sqrt(HD)

F32 = jnp.float32
BF16 = jnp.bfloat16
I32 = jnp.int32


def turn(step):
    return (step * STRIDE) % GEN


def iota(shape, dim):
    return lax.broadcasted_iota(I32, shape, dim)


def ones_where(cond):
    return jnp.where(cond, 1.0, 0.0).astype(BF16)


def dot(a, b):
    return jnp.dot(a, b, preferred_element_type=F32)


def dot_t(a, b):
    return lax.dot_general(a, b, (((1,), (1,)), ((), ())), preferred_element_type=F32)


def running(x, width):
    lane = iota(x.shape, 1) % width
    reach = 1
    while reach < width:
        x = x + jnp.where(lane >= reach, pltpu.roll(x, reach, 1), 0)
        reach *= 2
    return x


def first_two(match, values, width):
    hit = jnp.where(match, 1, 0)
    before = running(hit, width) - hit
    first = running(jnp.where(match & (before == 0), values, 0), width)
    second = running(jnp.where(match & (before == 1), values, 0), width)
    return first, second


def slot_owner(me, dest, seqs):
    src = iota((128, 128), 0)
    dst = iota((128, 128), 1)
    earlier = ones_where((src < dst) & (src // 64 == dst // 64))
    lane = iota((32, 128), 1)
    row = iota((32, 128), 0)
    match = dest == me
    before = dot(ones_where(match), earlier)
    first = match & (before < 0.5)
    second = match & (before > 0.5) & (before < 1.5)
    seqs = seqs.astype(F32) + 1.0
    own = dot(
        jnp.where(first, seqs, 0.0).astype(BF16), ones_where(dst == 2 * (src // 64))
    ) + dot(
        jnp.where(second, seqs, 0.0).astype(BF16), ones_where(dst == 2 * (src // 64) + 1)
    )
    spread = dot(own.astype(BF16), ones_where((dst % 4 == src) & (src < 4)))
    return jnp.sum(jnp.where(lane // 4 == row, spread, 0.0), axis=0, keepdims=True) - 1.0


def main_kernel(
    dest_ref, page_ref, seq_ref, pt_ref, len_ref, q_ref, x_hbm, w_hbm, k_hbm, v_hbm,
    att_ref, kv_ref,
    owner_s, own_s, own_v, lent_s, lent_v, qf, qlow, qhigh, outf, x_s, w_s, kaug, vaug, qaug, scores, probs, top_s,
    acc, mloc, num_s, den_s, cnt_s, sbuf, pbuf, mbuf, obuf,
    qsend, qrecv, rsend, rrecv, rf, kvsend, kvrecv, nk_s, nv_s,
    load_sem, tab_sem, plane_sem, qs_sem, qr_sem, rs_sem, rr_sem, ks_sem, kr_sem,
):
    me = lax.axis_index("gen")
    me_t = lax.axis_index("tp")
    mesh_id = pl.DeviceIdType.MESH

    loads = [
        pltpu.make_async_copy(x_hbm, x_s, load_sem.at[0]),
        pltpu.make_async_copy(w_hbm, w_s, load_sem.at[1]),
        pltpu.make_async_copy(k_hbm, kaug.at[:, :, pl.ds(0, HD)], load_sem.at[2]),
        pltpu.make_async_copy(v_hbm, vaug.at[:, :, pl.ds(0, HD)], load_sem.at[3]),
    ]
    for copy in loads:
        copy.start()

    barrier = pltpu.get_barrier_semaphore()

    plane = me // PLANE

    def near(u):
        return (me + u) % PLANE

    def greet(off, carry):
        pl.semaphore_signal(
            barrier, inc=1, device_id={"gen": plane * PLANE + near(off)}, device_id_type=mesh_id
        )
        return carry

    lax.fori_loop(1, PLANE, greet, 0, unroll=5)
    for off in range(1, TP):
        pl.semaphore_signal(
            barrier, inc=1, device_id={"tp": (me_t + off) % TP}, device_id_type=mesh_id
        )

    dest = dest_ref[...]
    own_v[0], own_v[1] = first_two(dest == me, seq_ref[...], 64)
    row = iota((32, 128), 0)
    mine = (row == me // 2) & (iota((32, 128), 1) // 64 == me % 2)
    my_dest = jnp.max(jnp.where(mine, dest, -1), axis=0, keepdims=True)
    my_page = jnp.max(jnp.where(mine, page_ref[...], 0), axis=0, keepdims=True)
    to_own = pltpu.make_async_copy(own_v, own_s, tab_sem.at[0])
    to_own.start()
    target = iota((GEN, 128), 0)
    my_page = jnp.broadcast_to(my_page, (GEN, 128))
    lent_v[0], lent_v[1] = first_two(my_dest == target, my_page, 128)
    to_lent = pltpu.make_async_copy(lent_v, lent_s, tab_sem.at[1])
    to_lent.start()

    qf[...] = q_ref[...].astype(F32)
    member_q = ones_where(iota((SEQ, 128), 0) == iota((SEQ, 128), 1))
    for r in range(HALF):
        if r < ROWS:
            q = qf[pl.ds(r, SEQ, stride=ROWS), :]
            qaug[r * SEQ:(r + 1) * SEQ, 0:HD] = q.astype(BF16)
            qaug[r * SEQ:(r + 1) * SEQ, HD:2 * HD] = member_q
        else:
            q = jnp.zeros((SEQ, HD), F32)
        qlow[:, r, :] = q
        qhigh[:, HALF + r, :] = q

    to_own.wait()

    crow = iota((CHUNK, 128), 0)

    @pl.loop(0, GEN // UNIT)
    def _(g):
        for u in range(UNIT):
            n = g * UNIT + u
            low = qlow[own_s[0, n // 2, n % 2 * 64 + 63]]
            high = qhigh[own_s[1, n // 2, n % 2 * 64 + 63]]
            qsend[n] = jnp.where(crow < HALF, low, high).astype(BF16)

    qrecv[0] = qsend[me]

    pl.semaphore_wait(barrier, PLANE - 1 + TP - 1 + plane)
    for j in range(PLANES):
        there = {"gen": j * PLANE + me % PLANE}

        @pl.when(j > plane)
        def _():
            pl.semaphore_signal(barrier, inc=1, device_id=there, device_id_type=mesh_id)

        @pl.when(j < plane)
        def _():
            pl.semaphore_signal(
                plane_sem.at[plane], inc=1, device_id=there, device_id_type=mesh_id
            )

    def q_copy(src, dst, sem, peer):
        return pltpu.make_async_remote_copy(
            src_ref=src, dst_ref=dst, send_sem=qs_sem, recv_sem=qr_sem.at[sem],
            device_id={"gen": peer}, device_id_type=mesh_id,
        )

    def r_copy(src, dst, sem, peer):
        return pltpu.make_async_remote_copy(
            src_ref=src, dst_ref=dst, send_sem=rs_sem, recv_sem=rr_sem.at[sem],
            device_id={"gen": peer}, device_id_type=mesh_id,
        )

    def kv_copy(src, dst, peer):
        return pltpu.make_async_remote_copy(
            src_ref=src, dst_ref=dst, send_sem=ks_sem, recv_sem=kr_sem,
            device_id={"tp": peer}, device_id_type=mesh_id,
        )

    def send_q(step, carry):
        peer = (me + turn(step)) % GEN
        q_copy(qsend.at[peer], qrecv.at[step], step // UNIT, peer).start()
        return carry

    def send_kv(off, carry):
        peer = (me_t + off) % TP
        kv_copy(kvsend.at[peer], kvrecv.at[off], peer).start()
        return carry

    def partial_kv():
        loads[0].wait()
        loads[1].wait()

        for h in range(TP):
            kvsend[h] = dot(x_s[...], w_s[:, h * 256:(h + 1) * 256]).astype(BF16)

    def mask():
        owner_s[...] = slot_owner(me, dest_ref[...], seq_ref[...])
        table_t = pt_ref[...].astype(F32)
        table_t = jnp.concatenate([table_t, table_t], axis=1)
        lens = len_ref[...].astype(F32)
        lens = jnp.concatenate([lens, lens], axis=1)
        first_row = iota((MAXP, 128), 0).astype(F32) * PAGE
        inside = jnp.clip(lens - first_row, 0.0, float(PAGE))
        page = iota((POOL, 128), 0).astype(F32)
        count = jnp.zeros((POOL, 128), F32)
        for m in range(MAXP):
            count = count + jnp.where(table_t[m:m + 1] == page, inside[m:m + 1], 0.0)
        cnt_s[...] = count

        place = iota((PAGE, 128), 0).astype(F32)

        @pl.loop(0, POOL // UNIT)
        def _(g):
            for u in range(UNIT):
                p = g * UNIT + u
                seen = place < cnt_s[pl.ds(p, 1), :]
                kaug[p, :, HD:2 * HD] = jnp.where(seen, 0.0, NEG).astype(BF16)
                vaug[p, :, HD:2 * HD] = jnp.ones((PAGE, HD), BF16)

        loads[2].wait()
        loads[3].wait()

    def attend(part):
        rows = slice(part * PART, (part + 1) * PART)
        qb = qaug[rows, :]
        top_s[...] = jnp.full((PART, 128), NEG, F32)

        @pl.loop(0, KEYS // 512)
        def _(c):
            for d in range(2):
                keys = kaug[pl.ds(c * 8 + d * 4, 4)].reshape(256, 2 * HD)
                s = dot_t(qb, keys)
                scores[2 * c + d] = s
                top_s[...] = jnp.maximum(top_s[...], jnp.maximum(s[:, :128], s[:, 128:]))

        top = jnp.max(top_s[...], axis=1, keepdims=True) * SCALE2
        top = jnp.broadcast_to(top, (PART, 128))
        mloc[rows, :] = top

        for c in range(KEYS // 256):
            for d in range(2):
                cols = slice(d * 128, (d + 1) * 128)
                p = jnp.exp2(scores[c, :, cols] * SCALE2 - mloc[rows, :])
                probs[:, c * 256 + d * 128:c * 256 + (d + 1) * 128] = p.astype(BF16)
        acc[rows, :] = dot(probs[...], vaug[...].reshape(KEYS, 2 * HD))

    early = plane < 2

    @pl.when(early)
    def _():
        partial_kv()
        lax.fori_loop(1, TP, send_kv, 0, unroll=7)
        mask()
        attend(0)
        attend(1)

    for j in range(1, PLANES):
        @pl.when(j > plane)
        def _():
            pl.semaphore_wait(plane_sem.at[j], 1)

    lax.fori_loop(1, GEN, send_q, 0, unroll=9)

    @pl.when(plane >= 2)
    def _():
        partial_kv()
        mask()
        attend(0)

    to_lent.wait()

    srow = iota((SUB, 128), 0) % CHUNK
    slane = iota((SUB, 128), 1)
    own_half = srow // HALF == slane // 64
    spot = (slane % 16 == srow % HALF) & (slane < 48) & (srow % HALF < ROWS)
    gather = ones_where(
        (iota((SUB, SUB), 0) % HALF == ROWS) & (iota((SUB, SUB), 0) // HALF == iota((SUB, SUB), 1) // HALF)
    )

    @pl.loop(0, GEN // WAVE)
    def _(g):
        @pl.when(g == 0)
        def _():
            q_copy(qsend.at[pl.ds(0, 7)], qrecv.at[pl.ds(1, 7)], 0, me).wait_recv()

        @pl.when(g > 0)
        def _():
            q_copy(qsend.at[pl.ds(0, 8)], qrecv.at[pl.ds(g * WAVE, 8)], 2 * g, me).wait_recv()

        q_copy(qsend.at[pl.ds(0, 8)], qrecv.at[pl.ds(g * WAVE + 8, 8)], 2 * g + 1, me).wait_recv()

        pages = []
        for u in range(WAVE):
            step = g * WAVE + u
            peer = (me + GEN - turn(step)) % GEN
            p0 = lent_s[0, peer, 127]
            p1 = lent_s[1, peer, 127]
            pages.append((p0, p1))
            keys = jnp.concatenate([kaug[p0, :, 0:HD], kaug[p1, :, 0:HD]], axis=0)
            sbuf[u * CHUNK:(u + 1) * CHUNK, :] = dot_t(qrecv[step], keys)
        for b in range(WAVE * CHUNK // SUB):
            rows = slice(b * SUB, (b + 1) * SUB)
            s = jnp.where(own_half, sbuf[rows, :] * SCALE2, NEG)
            top = jnp.broadcast_to(jnp.max(s, axis=1, keepdims=True), (SUB, 128))
            mbuf[rows, :] = top
            pbuf[rows, :] = jnp.exp2(s - top)
        for u in range(WAVE):
            p0, p1 = pages[u]
            vals = jnp.concatenate([vaug[p0], vaug[p1]], axis=0)
            obuf[u * CHUNK:(u + 1) * CHUNK, :] = dot(
                pbuf[u * CHUNK:(u + 1) * CHUNK, :].astype(BF16), vals
            )
        for b in range(WAVE * CHUNK // SUB):
            rows = slice(b * SUB, (b + 1) * SUB)
            total = obuf[rows, HD:]
            out = obuf[rows, :HD] / total
            mass = mbuf[rows, :] + jnp.log2(total)
            hi = mass.astype(BF16).astype(F32)
            mid = (mass - hi).astype(BF16).astype(F32)
            low = mass - hi - mid
            parts = jnp.where(slane < 16, hi, jnp.where(slane < 32, mid, low))
            parts = jnp.where(spot, parts, 0.0).astype(BF16)
            out = jnp.where(srow % HALF == ROWS, dot(gather, parts), out).astype(BF16)
            for j in range(SUB // CHUNK):
                rsend[g * WAVE + b * (SUB // CHUNK) + j] = out[j * CHUNK:(j + 1) * CHUNK]

        for u in range(WAVE):
            step = g * WAVE + u

            def send(step=step):
                peer = (me + GEN - turn(step)) % GEN
                r_copy(rsend.at[step], rrecv.at[step], step // UNIT, peer).start()

            if u == 0:
                pl.when(step > 0)(send)
            else:
                send()

    rrecv[0] = rsend[0]

    @pl.when(plane >= 2)
    def _():
        lax.fori_loop(1, TP, send_kv, 0, unroll=7)
        attend(1)

    kv_copy(kvsend.at[pl.ds(0, 7)], kvrecv.at[pl.ds(1, 7)], me_t).wait_recv()
    total = kvsend[me_t].astype(F32)
    for off in range(1, TP):
        total = total + kvrecv[off].astype(F32)
    fresh = total.astype(BF16)
    kv_ref[...] = fresh
    nk_s[...] = fresh[:, :HD].astype(F32)
    nv_s[...] = fresh[:, HD:].astype(F32)

    nk = [nk_s[pl.ds(i, SEQ, stride=2), :] for i in range(2)]
    nv = [nv_s[pl.ds(i, SEQ, stride=2), :] for i in range(2)]
    for r in range(ROWS):
        rows = slice(r * SEQ, (r + 1) * SEQ)
        q = qf[pl.ds(r, SEQ, stride=ROWS), :]
        new = [
            jnp.broadcast_to(jnp.sum(q * nk[i], axis=1, keepdims=True) * SCALE2, (SEQ, 128))
            for i in range(r % 2 + 1)
        ]
        local = mloc[rows, :]
        big = local
        for s in new:
            big = jnp.maximum(big, s)
        a = jnp.exp2(local - big)
        num = a * acc[rows, 0:HD]
        den = a * acc[rows, HD:2 * HD]
        for i, s in enumerate(new):
            e = jnp.exp2(s - big)
            num = num + e * nv[i]
            den = den + e
        mloc[rows, :] = big
        num_s[rows, :] = num
        den_s[rows, :] = den

    @pl.loop(0, GEN // UNIT)
    def _(g):
        @pl.when(g == 0)
        def _():
            r_copy(rsend.at[pl.ds(0, 7)], rrecv.at[pl.ds(1, 7)], 0, me).wait_recv()

        @pl.when(g > 0)
        def _():
            r_copy(rsend.at[pl.ds(0, 8)], rrecv.at[pl.ds(g * UNIT, 8)], g, me).wait_recv()

        for u in range(UNIT):
            step = g * UNIT + u
            peer = (me + turn(step)) % GEN
            rf[pl.ds(pl.multiple_of(peer * CHUNK, 8), CHUNK), :] = rrecv[step].astype(F32)

    pick = ones_where(
        (iota((16, 128), 1) % 16 == iota((16, 128), 0)) & (iota((16, 128), 1) < 48)
    )
    mass_t = dot_t(pick, rf[pl.ds(ROWS, 2 * GEN, stride=HALF), :].astype(BF16))
    member = owner_s[...] == iota((SEQ, 128), 0).astype(F32)
    ones = jnp.ones((2 * GEN, HD), BF16)
    for r in range(ROWS):
        rows = slice(r * SEQ, (r + 1) * SEQ)
        moved = jnp.where(member, mass_t[r:r + 1], NEG)
        before = mloc[rows, :]
        big = jnp.maximum(before, jnp.max(moved, axis=1, keepdims=True))
        f = jnp.exp2(moved - big)
        part = rf[pl.ds(r, 2 * GEN, stride=HALF), :].astype(BF16)
        part = jnp.concatenate([part, ones], axis=1)
        f_hi = f.astype(BF16)
        f_low = (f - f_hi.astype(F32)).astype(BF16)
        a = jnp.exp2(before - big)
        extra = dot(f_hi, part) + dot(f_low, part)
        num = a * num_s[rows, :] + extra[:, :HD]
        den = a * den_s[rows, :] + extra[:, HD:]
        outf[pl.ds(r, SEQ, stride=ROWS), :] = num / den

    att_ref[...] = outf[...].astype(BF16)

    q_copy(qsend.at[pl.ds(0, GEN - 1)], qrecv.at[pl.ds(0, GEN - 1)], 0, me).wait_send()
    r_copy(rsend.at[pl.ds(0, GEN - 1)], rrecv.at[pl.ds(0, GEN - 1)], 0, me).wait_send()
    kv_copy(kvsend.at[pl.ds(0, TP - 1)], kvrecv.at[pl.ds(0, TP - 1)], me_t).wait_send()


def copy_kernel(att_in, kv_in, att_out, kv_out, att_s, kv_s, sem):
    first = [
        pltpu.make_async_copy(att_in, att_s, sem.at[0]),
        pltpu.make_async_copy(kv_in, kv_s, sem.at[1]),
    ]
    second = [
        pltpu.make_async_copy(att_s, att_out, sem.at[2]),
        pltpu.make_async_copy(kv_s, kv_out, sem.at[3]),
    ]
    for copy in first:
        copy.start()
    for copy, onward in zip(first, second):
        copy.wait()
        onward.start()
    for copy in second:
        copy.wait()


def per_device(
    tokens_in, w_kv, queries, k_cache, v_cache, page_table, lengths, move_dest, move_page, move_seq
):
    vmem = pl.BlockSpec(memory_space=pltpu.VMEM)
    hbm = pl.BlockSpec(memory_space=pltpu.HBM)
    dma = pltpu.SemaphoreType.DMA
    att, new_kv = pl.pallas_call(
        main_kernel,
        out_shape=(
            jax.ShapeDtypeStruct((SEQ * ROWS, HD), BF16),
            jax.ShapeDtypeStruct((TOK, 256), BF16),
        ),
        in_specs=[vmem] * 6 + [hbm] * 4,
        out_specs=(vmem, vmem),
        scratch_shapes=[
            pltpu.VMEM((1, 128), F32),
            pltpu.SMEM((2, 32, 128), I32),
            pltpu.VMEM((2, 32, 128), I32),
            pltpu.SMEM((2, GEN, 128), I32),
            pltpu.VMEM((2, GEN, 128), I32),
            pltpu.VMEM((SEQ * ROWS, HD), F32),
            pltpu.VMEM((SEQ, CHUNK, HD), F32),
            pltpu.VMEM((SEQ, CHUNK, HD), F32),
            pltpu.VMEM((SEQ * ROWS, HD), F32),
            pltpu.VMEM((TOK, FEAT), BF16),
            pltpu.VMEM((FEAT, 2048), BF16),
            pltpu.VMEM((POOL, PAGE, 2 * HD), BF16),
            pltpu.VMEM((POOL, PAGE, 2 * HD), BF16),
            pltpu.VMEM((ROWS * SEQ, 2 * HD), BF16),
            pltpu.VMEM((KEYS // 256, PART, 256), F32),
            pltpu.VMEM((PART, KEYS), BF16),
            pltpu.VMEM((PART, 128), F32),
            pltpu.VMEM((ROWS * SEQ, 2 * HD), F32),
            pltpu.VMEM((ROWS * SEQ, 128), F32),
            pltpu.VMEM((ROWS * SEQ, 128), F32),
            pltpu.VMEM((ROWS * SEQ, 128), F32),
            pltpu.VMEM((POOL, 128), F32),
            pltpu.VMEM((WAVE * CHUNK, 128), F32),
            pltpu.VMEM((WAVE * CHUNK, 128), F32),
            pltpu.VMEM((WAVE * CHUNK, 128), F32),
            pltpu.VMEM((WAVE * CHUNK, 2 * HD), F32),
            pltpu.VMEM((GEN, CHUNK, HD), BF16),
            pltpu.VMEM((GEN, CHUNK, HD), BF16),
            pltpu.VMEM((GEN, CHUNK, HD), BF16),
            pltpu.VMEM((GEN, CHUNK, HD), BF16),
            pltpu.VMEM((GEN * CHUNK, HD), F32),
            pltpu.VMEM((TP, TOK, 256), BF16),
            pltpu.VMEM((TP, TOK, 256), BF16),
            pltpu.VMEM((TOK, HD), F32),
            pltpu.VMEM((TOK, HD), F32),
            dma((4,)), dma((2,)), pltpu.SemaphoreType.REGULAR((PLANES,)), dma(()), dma((GEN // UNIT,)), dma(()), dma((GEN // UNIT,)), dma(()), dma(()),
        ],
        compiler_params=pltpu.CompilerParams(
            collective_id=0, has_side_effects=True, vmem_limit_bytes=67043328
        ),
        name="decode",
    )(
        move_dest.reshape(32, 128), move_page.reshape(32, 128), move_seq.reshape(32, 128),
        page_table.T, lengths.reshape(1, SEQ),
        queries.transpose(0, 2, 1, 3).reshape(SEQ * ROWS, HD), tokens_in, w_kv,
        k_cache.reshape(POOL, PAGE, HD), v_cache.reshape(POOL, PAGE, HD),
    )
    shapes = (
        jax.ShapeDtypeStruct((SEQ * ROWS, HD), BF16),
        jax.ShapeDtypeStruct((TOK, 256), BF16),
    )
    att, new_kv = pl.pallas_call(
        copy_kernel,
        out_shape=shapes,
        in_specs=[hbm] * 2,
        out_specs=(hbm, hbm),
        scratch_shapes=[
            pltpu.VMEM((SEQ * ROWS, HD), BF16), pltpu.VMEM((TOK, 256), BF16), dma((4,)),
        ],
        compiler_params=pltpu.CompilerParams(vmem_limit_bytes=67043328),
        name="deliver",
    )(att, new_kv)
    attended = att.reshape(SEQ, 5, 2, HD).transpose(0, 2, 1, 3)
    return (attended, new_kv)


def solution(mesh):
    return jax.shard_map(
        per_device,
        mesh=mesh,
        in_specs=(
            P("gen", "tp"),
            P("tp", None),
            P("gen", None, "tp", None),
            P("gen", "tp", None, None),
            P("gen", "tp", None, None),
            P("gen", None),
            P("gen"),
            P(),
            P(),
            P(),
        ),
        out_specs=(P("gen", None, "tp", None), P("gen", "tp")),
        check_vma=False,
    )
```
